256 devices in a mesh: space: 128 (over y, z, x), dp: 2 (over core).
Axes of the slice: x: 4, y: 4, z: 8, core: 2. Of those that a mesh axis runs over, the one named last changes fastest.
Arguments:
- features: bfloat16 [1536, 8, 8, 512], P(('space', 'dp')), may hold values from -6 to 6
- grad_out: bfloat16 [1536, 8, 8, 512], P(('space', 'dp')), may hold values from -6 to 6
- occupancy: int32 [1536, 512], P(('space', 'dp')), may hold values 0 or 1
- weight: bfloat16 [3, 3, 3, 64, 64], replicated, may hold values from -0.15625 to 0.15625
- neighbours: int32 [1536, 26], P(('space', 'dp')), may hold values from 0 to 14, as said below
- send_rows: int32 [256, 4, 2], P(('space', 'dp')), may hold values from 0 to 6, as said below
Outputs:
- output: bfloat16 [1536, 8, 8, 512], P(('space', 'dp'))
- feature_grad: bfloat16 [1536, 8, 8, 512], P(('space', 'dp'))
- weight_grad: float32 [3, 3, 3, 64, 64], replicated
The draws below stay inside these ranges and needn't reach their ends.
Inputs may be any that keep to these rules, and one draw needn't show every extreme that they name: `neighbours`: A value below 6 names another block of the same device; 6 + k * 2 + j names slot j of list k of the device k sends from, that is the device 1 lower, 1 higher, 2 lower, 2 higher along space for k = 0, 1, 2, 3 (same dp index); 14 names no block. Every filled slot of a list sent to a device is named by some entry of that device, and no unfilled slot is named. `send_rows`: list k of a device holds the blocks it sends to the device 1 higher, 1 lower, 2 higher, 2 lower along space for k = 0, 1, 2, 3 (same dp index); 6 marks an unfilled slot, filled slots come first and name distinct blocks; lists to devices outside the axis are unfilled.
All inputs are finite; a program needn't handle non-finite values. No bound on the sum of `occupancy` on one device may be relied on, other than what follows from the above.
Results may differ from the reference program's by a relative error of at most 0.003.
Values may be sent and summed in bfloat16 or wider, within the bound.
No kernel may reach another device: no remote copies, remote signals or barrier semaphores. Data moves between devices by JAX's collectives and lax.ppermute only.
A program may use at most 128 MiB of HBM per device.

```python
import math
import jax
import jax.numpy as jnp
from jax import lax

EDGE = 8
C = 64
B_DEV = 6
CAP = 2
RANKS = 128
GROUPS = 256
BLOCKS = 1536
N_SPACE = 128
N_DP = 2


def plan_tables(key):
    base_key = jax.random.fold_in(key, 11)
    subkeys = jax.random.split(base_key, 6)
    groups = GROUPS
    blocks = B_DEV
    slot_count = CAP
    layers = groups // RANKS
    distances = jnp.array([1, -1, 2, -2], jnp.int32)
    device = jnp.arange(groups, dtype=jnp.int32)
    position = device // layers
    counts = jax.random.randint(subkeys[0], (groups, 4), (slot_count + 1) // 2, slot_count + 1)
    counts = counts.at[:, 0].set(slot_count)
    source = position[:, None] - distances[None, :]
    from_ok = (source >= 0) & (source < RANKS)
    target = position[:, None] + distances[None, :]
    to_ok = (target >= 0) & (target < RANKS)
    target_dev = jnp.clip(device[:, None] + distances[None, :] * layers, 0, groups - 1)
    target_count = counts[target_dev, jnp.arange(4)[None, :]]
    perm_keys = jax.random.split(subkeys[1], groups * 4)
    orders = jax.vmap(lambda subkey: jax.random.permutation(subkey, blocks))(perm_keys).reshape(groups, 4, blocks)[:, :, :slot_count]
    slot_ids = jnp.arange(slot_count)
    send_table = jnp.where(to_ok[:, :, None] & (slot_ids[None, None, :] < target_count[:, :, None]), orders, blocks)
    grid_shape = (groups, blocks, 26)
    kind_draw = jax.random.randint(subkeys[2], grid_shape, 0, 4)
    local_row = (jnp.arange(blocks)[None, :, None] + 1 + jax.random.randint(subkeys[3], grid_shape, 0, max(blocks - 1, 1))) % blocks
    peer_pick = jax.random.randint(subkeys[4], grid_shape, 0, 4)
    peer_count = counts[device[:, None, None], peer_pick]
    slot_pick = jax.random.randint(subkeys[5], grid_shape, 0, slot_count) % peer_count
    peer_ok = from_ok[device[:, None, None], peer_pick]
    remote = blocks + peer_pick * slot_count + slot_pick
    empty_row = blocks + 4 * slot_count
    beside = jnp.where(kind_draw == 0, empty_row, jnp.where((kind_draw == 1) & peer_ok, remote, local_row))
    all_slots = jnp.arange(4 * slot_count)
    slot_peer = all_slots // slot_count
    slot_place = all_slots % slot_count
    needed = from_ok[:, slot_peer] & (slot_place[None, :] < counts[:, slot_peer])
    fix_row = all_slots % blocks
    column = 25 - all_slots // blocks
    current = beside[:, fix_row, column]
    beside = beside.at[:, fix_row, column].set(jnp.where(needed, blocks + all_slots[None, :], current))
    return (beside.reshape(groups * blocks, 26).astype(jnp.int32), send_table.astype(jnp.int32))


def draw_neighbours(key, part):
    return plan_tables(key)[0]


def draw_send_rows(key, part):
    return plan_tables(key)[1]


def plant(values, rng, least, top_value):
    shape = values.shape
    index_at = [jax.random.randint(jax.random.fold_in(rng, axis), (), 0, shape[axis]) for axis in range(len(shape))]
    values = values.at[tuple(index_at)].set(least)
    longest = shape.index(max(shape))
    index_at[longest] = (index_at[longest] + 1) % shape[longest]
    return values.at[tuple(index_at)].set(top_value)


def steps_of(own_key, shape, shards, smallest, top_value):
    factor_of = 1.0
    for dim, blocks in shards:
        steps = jax.random.uniform(jax.random.fold_in(jax.random.fold_in(own_key, 6), dim), (blocks,), jnp.float32, smallest / len(shards), top_value / len(shards))
        factor_of = factor_of * jnp.repeat(jnp.exp(steps), shape[dim] // blocks).reshape((-1,) + (1,) * (len(shape) - 1 - dim))
    return factor_of


def centred(rng, extent, spread, bound, cuts=(), kind=jnp.bfloat16):
    factor_of = steps_of(rng, extent, cuts, -0.22, 0.18) if cuts else 1.0
    values = jax.random.normal(rng, extent, jnp.float32) * spread * factor_of
    return jnp.minimum(jnp.maximum(values, -bound), bound).astype(kind)


def setup_inputs(seed: int = 0) -> dict:
    key_list = jax.random.split(jax.random.key(seed), 7)
    return {
        "features": centred(key_list[0], (BLOCKS, EDGE, EDGE, EDGE * C), 1.0, 6.0, ((0, 256),)),
        "grad_out": centred(key_list[1], (BLOCKS, EDGE, EDGE, EDGE * C), 1.0, 6.0, ((0, 256),)),
        "occupancy": plant((jax.random.randint(key_list[2], (BLOCKS, EDGE ** 3), 0, 3) < 2).astype(jnp.int32), jax.random.fold_in(key_list[2], 1), 0, 1),
        "weight": centred(key_list[3], (3, 3, 3, C, C), (27 * C) ** -0.5, 0.15625),
        "neighbours": draw_neighbours(jax.random.fold_in(key_list[6], 71), 0),
        "send_rows": draw_send_rows(jax.random.fold_in(key_list[6], 71), 0),
    }


DISTANCES = (1, -1, 2, -2)
OFFSETS = [(step_x, step_y, step_z) for step_x in (-1, 0, 1) for step_y in (-1, 0, 1) for step_z in (-1, 0, 1) if (step_x, step_y, step_z) != (0, 0, 0)]
REACH = {-1: (7, 8, 0, 1), 0: (0, 8, 1, 9), 1: (0, 1, 9, 10)}

def matmul(left, right, left_dim, right_dim):
    dims = (((left_dim,), (right_dim,)), ((), ()))
    return lax.dot_general(left.astype(jnp.float32), right.astype(jnp.float32), dims, precision=lax.Precision.HIGHEST, preferred_element_type=jnp.float32)

def expand_mask(occupancy, channels):
    block_count = occupancy.shape[0]
    return jnp.repeat(occupancy.reshape(block_count, 8, 8, 8), channels, axis=3)

def band_weights(weight):
    channels = weight.shape[-1]
    zero_block = jnp.zeros((3, 3, channels, channels), weight.dtype)
    stacked = []
    for tap_in in range(4):
        parts = [weight[:, :, tap_in - out_pos] if 0 <= tap_in - out_pos <= 2 else zero_block for out_pos in range(2)]
        stacked.append(jnp.concatenate(parts, axis=3))
    return jnp.concatenate(stacked, axis=2)

def window_rows(slab, channels):
    block_count = slab.shape[0]
    stacked = jnp.stack([slab[..., 2 * channels * pair_num:2 * channels * pair_num + 4 * channels] for pair_num in range(4)], axis=3)
    return stacked.reshape(block_count * 256, 4 * channels)

def face_regions(table, channels):
    regions = []
    for step_x, step_y, step_z in OFFSETS:
        x_low, x_high = REACH[step_x][:2]
        y_low, y_high = REACH[step_y][:2]
        z_low, z_high = REACH[step_z][:2]
        regions.append(table[:, x_low:x_high, y_low:y_high, z_low * channels:z_high * channels])
    return regions

def assemble(regions, centre, index):
    pieces = {(0, 0, 0): centre}
    for slot_num, offset in enumerate(OFFSETS):
        pieces[offset] = jnp.take(regions[slot_num], index[:, slot_num], axis=0)
    planes = []
    for step_x in (-1, 0, 1):
        lines = []
        for step_y in (-1, 0, 1):
            lines.append(jnp.concatenate([pieces[step_x, step_y, step_z] for step_z in (-1, 0, 1)], axis=3))
        planes.append(jnp.concatenate(lines, axis=2))
    return jnp.concatenate(planes, axis=1)

def local_passes(padded, live_float, grads, banded):
    channels = banded.shape[-1] // 2
    block_count = padded.shape[0]
    grad_rows = grads.reshape(block_count * 256, 2 * channels)
    total = jnp.zeros((block_count * 256, 2 * channels), jnp.float32)
    dpad = jnp.zeros((block_count, 10, 10, 10 * channels), jnp.float32)
    dband = {}
    for shift_x in range(3):
        for shift_y in range(3):
            rows = window_rows(padded[:, shift_x:shift_x + 8, shift_y:shift_y + 8], channels)
            total = total + matmul(rows, banded[shift_x, shift_y], 1, 0)
            dband[shift_x, shift_y] = matmul(rows, grad_rows, 0, 0)
            back = matmul(grad_rows, banded[shift_x, shift_y], 1, 1).reshape(block_count, 8, 8, 4, 4 * channels)
            dslab = jnp.zeros((block_count, 8, 8, 10 * channels), jnp.float32)
            for pair_num in range(4):
                dslab = dslab.at[..., 2 * channels * pair_num:2 * channels * pair_num + 4 * channels].add(back[:, :, :, pair_num])
            dpad = dpad.at[:, shift_x:shift_x + 8, shift_y:shift_y + 8].add(dslab)
    output = (total.reshape(block_count, 8, 8, 8 * channels) * live_float).astype(jnp.bfloat16)

    def tap(shift_x, shift_y, shift_z):
        full = dband[shift_x, shift_y]
        terms = [full[(out_pos + shift_z) * channels:(out_pos + shift_z + 1) * channels, out_pos * channels:(out_pos + 1) * channels] for out_pos in range(2)]
        return terms[0] + terms[1]
    dweight = jnp.stack([jnp.stack([jnp.stack([tap(shift_x, shift_y, shift_z) for shift_z in range(3)]) for shift_y in range(3)]) for shift_x in range(3)])
    return (output, dpad, dweight)

def reference(features, grad_out, occupancy, weight, neighbours, send_rows):
    channels = weight.shape[-1]
    blocks = B_DEV
    slot_count = CAP
    groups = N_SPACE * N_DP
    live = expand_mask(occupancy, channels) == 1
    shown = jnp.where(live, features, jnp.zeros_like(features))
    masked_grad = jnp.where(live, grad_out, jnp.zeros_like(grad_out))
    live_float = live.astype(jnp.float32)
    table = jnp.concatenate([shown, jnp.zeros((1, 8, 8, 8 * channels), jnp.bfloat16)], axis=0)
    device = jnp.arange(groups, dtype=jnp.int32)
    position = device // N_DP
    distance = jnp.array(DISTANCES, dtype=jnp.int32)
    source_space = position[:, None] - distance[None, :]
    source_ok = (source_space >= 0) & (source_space < N_SPACE)
    source_dev = jnp.clip(device[:, None] - distance[None, :] * N_DP, 0, groups - 1).astype(jnp.int32)
    sent = send_rows[source_dev, jnp.arange(4, dtype=jnp.int32)[None, :]]
    recv_global = jnp.where(source_ok[:, :, None] & (sent < blocks), source_dev[:, :, None] * blocks + sent, BLOCKS)
    recv_flat = recv_global.reshape(groups, 4 * slot_count).astype(jnp.int32)
    local_ids = neighbours.reshape(groups, blocks, 26)
    remote_pos = jnp.clip(local_ids - blocks, 0, 4 * slot_count - 1).astype(jnp.int32)
    remote_ids = recv_flat[device[:, None, None], remote_pos]
    global_ids = jnp.where(local_ids < blocks, device[:, None, None] * blocks + local_ids, jnp.where(local_ids == blocks + 4 * slot_count, BLOCKS, remote_ids)).astype(jnp.int32)
    regions = face_regions(table, channels)
    banded = band_weights(weight)

    def step(carry, device_num):
        accum, dsum = carry
        start = (device_num * blocks).astype(jnp.int32)
        centre = lax.dynamic_slice_in_dim(shown, start, blocks, 0)
        index = lax.dynamic_index_in_dim(global_ids, device_num, 0, keepdims=False)
        grads = lax.dynamic_slice_in_dim(masked_grad, start, blocks, 0)
        live_here = lax.dynamic_slice_in_dim(live_float, start, blocks, 0)
        padded = assemble(regions, centre, index)
        output, dpad, dweight = local_passes(padded, live_here, grads, banded)
        inner = dpad[:, 1:9, 1:9, channels:9 * channels]
        accum = lax.dynamic_update_slice_in_dim(accum, lax.dynamic_slice_in_dim(accum, start, blocks, 0) + inner, start, 0)
        for slot_num, offset in enumerate(OFFSETS):
            xn0, xn1, xp0, xp1 = REACH[offset[0]]
            yn0, yn1, yp0, yp1 = REACH[offset[1]]
            zn0, zn1, zp0, zp1 = REACH[offset[2]]
            accum = accum.at[index[:, slot_num], xn0:xn1, yn0:yn1, zn0 * channels:zn1 * channels].add(dpad[:, xp0:xp1, yp0:yp1, zp0 * channels:zp1 * channels])
        return ((accum, dsum + dweight), output)
    init = (jnp.zeros((BLOCKS + 1, 8, 8, 8 * channels), jnp.float32), jnp.zeros((3, 3, 3, channels, channels), jnp.float32))
    (accum, dsum), outputs = lax.scan(step, init, jnp.arange(groups, dtype=jnp.int32))
    output = outputs.reshape(BLOCKS, 8, 8, 8 * channels)
    feature_grad = (accum[:BLOCKS] * live_float).astype(jnp.bfloat16)
    weight_grad = dsum * (1.0 / math.sqrt(BLOCKS * 512))
    return (output, feature_grad, weight_grad)
```

```python
import math

import jax
import jax.numpy as jnp
from jax import lax
from jax.experimental import pallas as pl
from jax.experimental.pallas import tpu as pltpu
from jax.sharding import PartitionSpec as P

DISTANCES = (1, -1, 2, -2)
OFFSETS = [
    (step_x, step_y, step_z)
    for step_x in (-1, 0, 1)
    for step_y in (-1, 0, 1)
    for step_z in (-1, 0, 1)
    if (step_x, step_y, step_z) != (0, 0, 0)
]
SLOT_OF = {offset: num for num, offset in enumerate(OFFSETS)}
BF16 = jnp.bfloat16
F32 = jnp.float32
NB = 6
CAP = 2
NT = NB + 4 * CAP + 1


def shifted(block, axis, distance):
    devices = range(lax.axis_size(axis))
    route = [(i - distance, i) for i in devices if i - distance in devices]
    return lax.ppermute(block, axis, route)


def dot(left, right, left_dim, right_dim):
    dims = (((left_dim,), (right_dim,)), ((), ()))
    return lax.dot_general(left, right, dims, preferred_element_type=F32)


def live_rows(occ):
    z = lax.broadcasted_iota(jnp.int32, (8, 512), 0)
    lane = lax.broadcasted_iota(jnp.int32, (8, 512), 1)
    spread = (lane // 64 == z).astype(F32).astype(BF16)
    return dot(occ, spread, 1, 0)


def lanes(t):
    return slice(128 * t, 128 * t + 128)


def prep_kernel(feat, grad, occ, send, shown, g, s0, s1, s2, s3, live):
    live[...] = live_rows(occ[...])
    for x in range(8):
        for pair in range(NB // 2):
            parts = []
            for b in (2 * pair, 2 * pair + 1):
                on = live[x * 48 + b * 8 : x * 48 + b * 8 + 8, :] > 0.5
                f = feat[b, x].astype(F32)
                shown[b, x] = jnp.where(on, f, 0.0).astype(BF16)
                parts.append(jnp.where(on, grad[b, x].astype(F32), 0.0))
            g[x, 16 * pair : 16 * pair + 16, :] = jnp.concatenate(parts, axis=0).astype(BF16)
    for k, out in enumerate((s0, s1, s2, s3)):
        for j in range(CAP):
            row = jnp.minimum(send[k, j], NB - 1)
            out[j] = shown[row]


def dgrad_kernel(g, wp, nbr, rloc, r0, r1, r2, r3, gext, wbt, dsc, acc):
    gext[0:96, :] = jnp.zeros((96, 768), BF16)
    gext[480:576, :] = jnp.zeros((96, 768), BF16)
    gext[96:480, 0:128] = jnp.zeros((384, 128), BF16)
    gext[96:480, 640:768] = jnp.zeros((384, 128), BF16)
    for x in range(8):
        gext[96 + 48 * x : 144 + 48 * x, 128:640] = g[x]
    for a in range(3):
        for c in range(3):
            for o in range(2):
                for s in range(2):
                    row = c * 128 + (1 - o) * 64
                    wbt[row : row + 64, a * 256 + s * 128 : a * 256 + s * 128 + 128] = wp[
                        (a * 3 + c) * 4 + o + 2 - 2 * s
                    ]
    for q in range(5):
        left = jnp.concatenate(
            [
                gext[(2 - a) * 48 : (2 - a) * 48 + 480, 128 * q : 128 * q + 256]
                for a in range(3)
            ],
            axis=1,
        )
        dsc[q] = dot(left, wbt[...], 1, 1)
    acc[...] = jnp.zeros((NT * 8, 8, 512), F32)
    low = lax.broadcasted_iota(jnp.int32, (8, 128), 1) < 64
    sub = lax.broadcasted_iota(jnp.int32, (8, 128), 0)

    def add_rows(b, offset, xs, tiles):
        def target(oz):
            if (offset[0], offset[1], oz) == (0, 0, 0):
                return b * 8 + xs
            return nbr[b, SLOT_OF[offset[0], offset[1], oz]] * 8 + xs

        row = target(0)
        for t in range(4):
            acc[row, :, lanes(t)] += tiles[t]
        row = target(1)
        acc[row, :, lanes(0)] += jnp.where(low, tiles[4], 0.0)
        row = target(-1)
        acc[row, :, lanes(3)] += jnp.where(low, 0.0, tiles[4])

    def group(xx, ox, xs):
        for b in range(NB):
            base = pl.multiple_of(xx * 48 + b * 8, 8)
            z = []
            for c in range(3):
                d = [dsc[t, pl.ds(base, 8), lanes(c)] for t in range(5)]
                z.append([jnp.where(low, d[t], d[(t + 1) % 5]) for t in range(5)])
            up = [pltpu.roll(v, 7, 0) for v in z[0]]
            down = [pltpu.roll(v, 1, 0) for v in z[2]]
            inner = [
                z[1][t] + jnp.where(sub < 7, up[t], 0.0) + jnp.where(sub > 0, down[t], 0.0)
                for t in range(5)
            ]
            add_rows(b, (ox, 0), xs, inner)
            add_rows(b, (ox, -1), xs, [jnp.where(sub == 7, v, 0.0) for v in up])
            add_rows(b, (ox, 1), xs, [jnp.where(sub == 0, v, 0.0) for v in down])

    group(0, -1, 7)

    def middle(x, carry):
        group(x + 1, 0, x)
        return carry

    lax.fori_loop(0, 8, middle, 0)
    group(9, 1, 0)
    rloc[...] = acc[0 : NB * 8]
    for k, out in enumerate((r0, r1, r2, r3)):
        for j in range(CAP):
            for x in range(8):
                out[j, x] = acc[(NB + CAP * k + j) * 8 + x].astype(BF16)


def conv_kernel(
    shown, a0, a1, a2, a3, g, wp, occ, nbr, out, dwp,
    table, px, wf, gsc, gext, dsc, live, sems,
):
    copies = [pltpu.make_async_copy(shown, table.at[0:NB], sems.at[0])]
    for k, src in enumerate((a0, a1, a2, a3)):
        start = NB + CAP * k
        copies.append(
            pltpu.make_async_copy(src, table.at[start : start + CAP], sems.at[k + 1])
        )
    for copy in copies:
        copy.start()
    low = lax.broadcasted_iota(jnp.int32, (8, 128), 1) < 64
    sub = lax.broadcasted_iota(jnp.int32, (8, 128), 0)
    zero = jnp.zeros((8, 128), F32)
    table[NT - 1] = jnp.zeros((8, 8, 512), BF16)
    live[...] = live_rows(occ[...])
    for a in range(3):
        for c in range(3):
            for n, t in enumerate((1, 2, 3, 0)):
                row = a * 256 + n * 64
                wf[row : row + 64, lanes(c)] = wp[(a * 3 + c) * 4 + t]
    gext[0:128, :] = jnp.zeros((128, 1536), BF16)
    gext[640:768, :] = jnp.zeros((128, 1536), BF16)

    def fill_g(x, carry):
        for p in range(4):
            cols = [p * 384 + c * 128 for c in range(3)]
            h_low, h_high = zero, zero
            base = pl.multiple_of((x + 2) * 64, 64)
            for pair in range(NB // 2):
                both = g[x, 16 * pair : 16 * pair + 16, lanes(p)]
                both32 = both.astype(F32)
                ups, downs = [], []
                for half in range(2):
                    b = 2 * pair + half
                    v = both32[8 * half : 8 * half + 8]
                    ups.append(jnp.where(sub < 7, pltpu.roll(v, 7, 0), 0.0))
                    downs.append(jnp.where(sub > 0, pltpu.roll(v, 1, 0), 0.0))
                    h_low = jnp.where(sub == b, pltpu.roll(v, b, 0) if b else v, h_low)
                    h_high = jnp.where(sub == b, pltpu.roll(v, b + 1, 0), h_high)
                rows = pl.ds(pl.multiple_of(base + 16 * pair, 16), 16)
                gext[rows, cols[0] : cols[0] + 128] = jnp.concatenate(ups, 0).astype(BF16)
                gext[rows, cols[1] : cols[1] + 128] = both
                gext[rows, cols[2] : cols[2] + 128] = jnp.concatenate(downs, 0).astype(BF16)
            rows = pl.ds(pl.multiple_of(base + 48, 16), 16)
            gext[rows, cols[0] : cols[0] + 128] = jnp.concatenate([h_low, zero], 0).astype(BF16)
            gext[rows, cols[1] : cols[1] + 128] = jnp.zeros((16, 128), BF16)
            gext[rows, cols[2] : cols[2] + 128] = jnp.concatenate([zero, h_high], 0).astype(BF16)
        return carry

    lax.fori_loop(0, 8, fill_g, 0)
    for copy in copies:
        copy.wait()

    def windows(tiles):
        merged = [
            jnp.where(low, tiles[p + 1], tiles[(p + 4) % 5]) for p in range(4)
        ]
        return [v for p in range(4) for v in (tiles[p], merged[p])]

    def five(b, ox, oy, xs):
        def source(oz):
            if (ox, oy, oz) == (0, 0, 0):
                return table[b, xs].astype(F32)
            return table[nbr[b, SLOT_OF[ox, oy, oz]], xs].astype(F32)

        centre, after, before = source(0), source(1), source(-1)
        tiles = [centre[:, lanes(t)] for t in range(4)]
        return tiles + [jnp.where(low, after[:, lanes(0)], before[:, lanes(3)])]

    def fill_plane(xx, ox, xs):
        base = pl.multiple_of(xx * 64, 64)
        h_low, h_high = [zero] * 5, [zero] * 5
        for pair in range(NB // 2):
            wins = []
            for b in (2 * pair, 2 * pair + 1):
                wins.append(windows(five(b, ox, 0, xs)))
                v = five(b, ox, -1, xs)
                h_low = [
                    jnp.where(sub == b, pltpu.roll(v[t], b + 1, 0), h_low[t]) for t in range(5)
                ]
                v = five(b, ox, 1, xs)
                h_high = [
                    jnp.where(sub == b, pltpu.roll(v[t], b, 0) if b else v[t], h_high[t])
                    for t in range(5)
                ]
            rows = pl.ds(pl.multiple_of(base + 16 * pair, 16), 16)
            for n in range(8):
                px[rows, lanes(n)] = jnp.concatenate([wins[0][n], wins[1][n]], 0).astype(BF16)
        wins = [windows(h_low), windows(h_high)]
        rows = pl.ds(pl.multiple_of(base + 48, 16), 16)
        for n in range(8):
            px[rows, lanes(n)] = jnp.concatenate([wins[0][n], wins[1][n]], 0).astype(BF16)

    fill_plane(0, -1, 7)

    def middle_fill(x, carry):
        fill_plane(x + 1, 0, x)
        return carry

    lax.fori_loop(0, 8, middle_fill, 0)
    fill_plane(9, 1, 0)

    for p in range(4):
        right = jnp.concatenate(
            [
                gext[(2 - a) * 64 : (2 - a) * 64 + 640, p * 384 : p * 384 + 384]
                for a in range(3)
            ],
            axis=1,
        )
        part = dot(px[:, 256 * p : 256 * p + 256], right, 0, 0)
        if p == 0:
            dsc[...] = part
        else:
            dsc[...] += part
    low64 = lax.broadcasted_iota(jnp.int32, (64, 128), 1) < 64
    row_of = (192, 0, 64, 128)
    taps = [(a, c, e) for a in range(3) for c in range(3) for e in range(3)]

    def tap_parts(tap):
        a, c, e = tap
        col = a * 384 + c * 128
        first = dsc[row_of[e] : row_of[e] + 64, col : col + 128]
        second = dsc[row_of[e + 1] : row_of[e + 1] + 64, col : col + 128]
        return first, second

    for n in range(14):
        first, second = tap_parts(taps[2 * n])
        left = first + pltpu.roll(second, 64, 1)
        if 2 * n + 1 < 27:
            first, second = tap_parts(taps[2 * n + 1])
            right = second + pltpu.roll(first, 64, 1)
        else:
            right = jnp.zeros((64, 128), F32)
        dwp[64 * n : 64 * n + 64, :] = jnp.where(low64, left, right)
    dwp[896:1024, :] = jnp.zeros((128, 128), F32)

    for p in range(4):
        left = jnp.concatenate(
            [px[64 * a : 64 * a + 512, 256 * p : 256 * p + 256] for a in range(3)], axis=1
        )
        gsc[p] = dot(left, wf[...], 1, 0)

    def finish(x, carry):
        base = pl.multiple_of(x * 64, 64)
        for p in range(4):
            lo_rows = gsc[p, pl.ds(pl.multiple_of(base + 48, 8), 8), lanes(0)]
            hi_rows = gsc[p, pl.ds(pl.multiple_of(base + 56, 8), 8), lanes(2)]
            for b in range(NB):
                rows = pl.ds(pl.multiple_of(base + 8 * b, 8), 8)
                v = [gsc[p, rows, lanes(c)] for c in range(3)]
                lo = pltpu.roll(lo_rows, (8 - b) % 8, 0) if b else lo_rows
                hi = pltpu.roll(hi_rows, 7 - b, 0)
                total = (
                    v[1]
                    + jnp.where(sub > 0, pltpu.roll(v[0], 1, 0), lo)
                    + jnp.where(sub < 7, pltpu.roll(v[2], 7, 0), hi)
                )
                on = live[pl.ds(pl.multiple_of(x * 48 + 8 * b, 8), 8), lanes(p)]
                out[b, x, :, lanes(p)] = (total * on).astype(BF16)
        return carry

    lax.fori_loop(0, 8, finish, 0)


def final_kernel(rloc, a0, a1, a2, a3, occ, send, out, acc, live):
    live[...] = live_rows(occ[...])
    acc[...] = rloc[...]
    for k, src in enumerate((a0, a1, a2, a3)):
        for j in range(CAP):
            row = send[k, j]

            @pl.when(row < NB)
            def _(src=src, j=j, row=row):
                for x in range(8):
                    acc[row * 8 + x] += src[j, x].astype(F32)

    for x in range(8):
        for b in range(NB):
            on = live[x * 48 + b * 8 : x * 48 + b * 8 + 8, :]
            out[b, x] = (acc[b * 8 + x] * on).astype(BF16)


def sum_kernel(parts, out, *, scale):
    out[...] = jnp.broadcast_to(
        (jnp.sum(parts[...], axis=0) * scale)[None], out.shape
    )


def unpack_kernel(packed, out):
    for n in range(14):
        tile = packed[64 * n : 64 * n + 64, :]
        out[2 * n] = tile[:, 0:64]
        if 2 * n + 1 < 27:
            out[2 * n + 1] = pltpu.roll(tile, 64, 1)[:, 0:64]


VM = pl.BlockSpec(memory_space=pltpu.VMEM)
SM = pl.BlockSpec(memory_space=pltpu.SMEM)
ANY = pl.BlockSpec(memory_space=pl.ANY)
BLOCK = jax.ShapeDtypeStruct((NB, 8, 8, 512), BF16)
SEND = jax.ShapeDtypeStruct((CAP, 8, 8, 512), BF16)


def on_device(features, grad_out, occupancy, weight, neighbours, send_rows):
    send_plan = send_rows[0]
    occ = occupancy.astype(BF16).reshape(NB, 8, 8, 8)
    occ = jnp.transpose(occ, (1, 0, 2, 3)).reshape(NB * 64, 8)
    w = weight.reshape(9, 3, 64, 64)
    none = jnp.zeros((9, 1, 64, 64), BF16)
    wp = jnp.concatenate(
        [jnp.concatenate([w, none], axis=1), jnp.concatenate([none, w], axis=1)], axis=3
    ).reshape(36, 64, 128)

    shown, g, *sends = pl.pallas_call(
        prep_kernel,
        out_shape=(BLOCK, jax.ShapeDtypeStruct((8, 48, 512), BF16), SEND, SEND, SEND, SEND),
        in_specs=[VM, VM, VM, SM],
        out_specs=[VM] * 6,
        scratch_shapes=[pltpu.VMEM((NB * 64, 512), F32)],
        name="prep",
    )(features, grad_out, occ, send_plan)
    arrived = [shifted(s, "space", d) for s, d in zip(sends, DISTANCES)]
    rloc, *backs = pl.pallas_call(
        dgrad_kernel,
        out_shape=(jax.ShapeDtypeStruct((NB * 8, 8, 512), F32), SEND, SEND, SEND, SEND),
        in_specs=[VM, VM, SM],
        out_specs=[VM] * 5,
        scratch_shapes=[
            pltpu.VMEM((576, 768), BF16),
            pltpu.VMEM((384, 768), BF16),
            pltpu.VMEM((5, 480, 384), F32),
            pltpu.VMEM((NT * 8, 8, 512), F32),
        ],
        name="dgrad",
    )(g, wp, neighbours)
    returned = [shifted(s, "space", -d) for s, d in zip(backs, DISTANCES)]
    output, dwp = pl.pallas_call(
        conv_kernel,
        out_shape=(BLOCK, jax.ShapeDtypeStruct((1024, 128), F32)),
        in_specs=[ANY, ANY, ANY, ANY, ANY, VM, VM, VM, SM],
        out_specs=[VM] * 2,
        scratch_shapes=[
            pltpu.VMEM((NT, 8, 8, 512), BF16),
            pltpu.VMEM((640, 1024), BF16),
            pltpu.VMEM((768, 384), BF16),
            pltpu.VMEM((4, 512, 384), F32),
            pltpu.VMEM((768, 1536), BF16),
            pltpu.VMEM((256, 1152), F32),
            pltpu.VMEM((NB * 64, 512), F32),
            pltpu.SemaphoreType.DMA((5,)),
        ],
        name="conv",
    )(shown, *arrived, g, wp, occ, neighbours)

    count = lax.axis_size("space") * lax.axis_size("dp")
    scale = 1.0 / math.sqrt(count * NB * 512)
    axes = ("space", "dp")
    rows = 1024 // count
    parts = lax.all_to_all(dwp.reshape(count, rows, 128), axes, 0, 0, tiled=True)
    total = pl.pallas_call(
        lambda parts, out: sum_kernel(parts, out, scale=scale),
        out_shape=jax.ShapeDtypeStruct((count, rows, 128), F32),
        in_specs=[VM],
        out_specs=VM,
        name="sum",
    )(parts)
    packed = lax.all_to_all(total, axes, 0, 0, tiled=True).reshape(1024, 128)
    weight_grad = pl.pallas_call(
        unpack_kernel,
        out_shape=jax.ShapeDtypeStruct((27, 64, 64), F32),
        in_specs=[VM],
        out_specs=VM,
        name="unpack",
    )(packed).reshape(3, 3, 3, 64, 64)
    feature_grad = pl.pallas_call(
        final_kernel,
        out_shape=BLOCK,
        in_specs=[VM, VM, VM, VM, VM, VM, SM],
        out_specs=VM,
        scratch_shapes=[
            pltpu.VMEM((NB * 8, 8, 512), F32),
            pltpu.VMEM((NB * 64, 512), F32),
        ],
        name="final",
    )(rloc, *returned, occ, send_plan)
    return (output, feature_grad, weight_grad)


def solution(mesh):
    return jax.shard_map(
        on_device,
        mesh=mesh,
        in_specs=(
            P(("space", "dp"), None, None, None),
            P(("space", "dp"), None, None, None),
            P(("space", "dp"), None),
            P(),
            P(("space", "dp"), None),
            P(("space", "dp"), None, None),
        ),
        out_specs=(P(("space", "dp"), None, None, None), P(("space", "dp"), None, None, None), P()),
        check_vma=False,
    )
```

```python
import math

import jax
import jax.numpy as jnp
from jax import lax
from jax.experimental import pallas as pl
from jax.experimental.pallas import tpu as pltpu
from jax.sharding import PartitionSpec as P

DISTANCES = (1, -1, 2, -2)
OFFSETS = [
    (step_x, step_y, step_z)
    for step_x in (-1, 0, 1)
    for step_y in (-1, 0, 1)
    for step_z in (-1, 0, 1)
    if (step_x, step_y, step_z) != (0, 0, 0)
]
SLOT_OF = {offset: num for num, offset in enumerate(OFFSETS)}
BF16 = jnp.bfloat16
F32 = jnp.float32
NB = 6
CAP = 2
NT = NB + 4 * CAP + 1


def shifted(block, axis, distance):
    devices = range(lax.axis_size(axis))
    route = [(i - distance, i) for i in devices if i - distance in devices]
    return lax.ppermute(block, axis, route)


def dot(left, right, left_dim, right_dim):
    dims = (((left_dim,), (right_dim,)), ((), ()))
    return lax.dot_general(left, right, dims, preferred_element_type=F32)


def live_block(occ_row):
    voxel = lax.broadcasted_iota(jnp.int32, (64, 512), 1)
    line = lax.broadcasted_iota(jnp.int32, (64, 512), 0)
    left = jnp.where(voxel // 8 == line, jnp.broadcast_to(occ_row, (64, 512)), 0)
    voxel = lax.broadcasted_iota(jnp.int32, (512, 512), 0)
    lane = lax.broadcasted_iota(jnp.int32, (512, 512), 1)
    spread = jnp.where(voxel % 8 == lane // 64, 1.0, 0.0)
    return dot(left.astype(F32).astype(BF16), spread.astype(BF16), 1, 0)


def lanes(t):
    return slice(128 * t, 128 * t + 128)


def prep_kernel(feat, grad, occ, send, shown, g, live, s0, s1, s2, s3, mask):
    for b in range(NB):
        mask[64 * b : 64 * b + 64, :] = live_block(occ[b : b + 1, :])
    for x in range(8):
        for pair in range(NB // 2):
            parts = []
            for b in (2 * pair, 2 * pair + 1):
                on = mask[b * 64 + x * 8 : b * 64 + x * 8 + 8, :]
                live[b, x] = on.astype(BF16)
                f = feat[b, x].astype(F32)
                shown[b, x] = jnp.where(on > 0.5, f, 0.0).astype(BF16)
                parts.append(jnp.where(on > 0.5, grad[b, x].astype(F32), 0.0))
            g[x, 16 * pair : 16 * pair + 16, :] = jnp.concatenate(parts, axis=0).astype(BF16)
    for k, out in enumerate((s0, s1, s2, s3)):
        for j in range(CAP):
            row = jnp.minimum(send[0, k, j], NB - 1)
            out[j] = shown[row]


def dgrad_kernel(g, wp, nbr, rloc, r0, r1, r2, r3, gext, wbt, dsc, acc):
    gext[0:96, :] = jnp.zeros((96, 768), BF16)
    gext[480:576, :] = jnp.zeros((96, 768), BF16)
    gext[96:480, 0:128] = jnp.zeros((384, 128), BF16)
    gext[96:480, 640:768] = jnp.zeros((384, 128), BF16)
    for x in range(8):
        gext[96 + 48 * x : 144 + 48 * x, 128:640] = g[x]
    for a in range(3):
        for c in range(3):
            for o in range(2):
                for s in range(2):
                    row = c * 128 + (1 - o) * 64
                    wbt[row : row + 64, a * 256 + s * 128 : a * 256 + s * 128 + 128] = wp[
                        (a * 3 + c) * 4 + o + 2 - 2 * s
                    ]
    for q in range(5):
        left = jnp.concatenate(
            [
                gext[(2 - a) * 48 : (2 - a) * 48 + 480, 128 * q : 128 * q + 256]
                for a in range(3)
            ],
            axis=1,
        )
        dsc[q] = dot(left, wbt[...], 1, 1)
    acc[...] = jnp.zeros((NT * 8, 8, 512), F32)
    low = lax.broadcasted_iota(jnp.int32, (8, 128), 1) < 64
    sub = lax.broadcasted_iota(jnp.int32, (8, 128), 0)

    def add_rows(b, offset, xs, tiles):
        def target(oz):
            if (offset[0], offset[1], oz) == (0, 0, 0):
                return b * 8 + xs
            return nbr[b, SLOT_OF[offset[0], offset[1], oz]] * 8 + xs

        row = target(0)
        for t in range(4):
            acc[row, :, lanes(t)] += tiles[t]
        row = target(1)
        acc[row, :, lanes(0)] += jnp.where(low, tiles[4], 0.0)
        row = target(-1)
        acc[row, :, lanes(3)] += jnp.where(low, 0.0, tiles[4])

    def group(xx, ox, xs):
        for b in range(NB):
            base = pl.multiple_of(xx * 48 + b * 8, 8)
            z = []
            for c in range(3):
                d = [dsc[t, pl.ds(base, 8), lanes(c)] for t in range(5)]
                z.append([jnp.where(low, d[t], d[(t + 1) % 5]) for t in range(5)])
            up = [pltpu.roll(v, 7, 0) for v in z[0]]
            down = [pltpu.roll(v, 1, 0) for v in z[2]]
            inner = [
                z[1][t] + jnp.where(sub < 7, up[t], 0.0) + jnp.where(sub > 0, down[t], 0.0)
                for t in range(5)
            ]
            add_rows(b, (ox, 0), xs, inner)
            add_rows(b, (ox, -1), xs, [jnp.where(sub == 7, v, 0.0) for v in up])
            add_rows(b, (ox, 1), xs, [jnp.where(sub == 0, v, 0.0) for v in down])

    group(0, -1, 7)

    def middle(x, carry):
        group(x + 1, 0, x)
        return carry

    lax.fori_loop(0, 8, middle, 0)
    group(9, 1, 0)
    rloc[...] = acc[0 : NB * 8]
    for k, out in enumerate((r0, r1, r2, r3)):
        for j in range(CAP):
            for x in range(8):
                out[j, x] = acc[(NB + CAP * k + j) * 8 + x].astype(BF16)


def wgrad_kernel(shown, a0, a1, a2, a3, after, g, nbr, px, dwp, table, gext, dsc, sems):
    copies = [pltpu.make_async_copy(shown, table.at[0:NB], sems.at[0])]
    for k, src in enumerate((a0, a1, a2, a3)):
        start = NB + CAP * k
        copies.append(
            pltpu.make_async_copy(src, table.at[start : start + CAP], sems.at[k + 1])
        )
    for copy in copies:
        copy.start()
    low = lax.broadcasted_iota(jnp.int32, (8, 128), 1) < 64
    sub = lax.broadcasted_iota(jnp.int32, (8, 128), 0)
    zero = jnp.zeros((8, 128), F32)
    table[NT - 1] = jnp.zeros((8, 8, 512), BF16)
    gext[0:128, :] = jnp.zeros((128, 1536), BF16)
    gext[640:768, :] = jnp.zeros((128, 1536), BF16)

    def fill_g(x, carry):
        for p in range(4):
            cols = [p * 384 + c * 128 for c in range(3)]
            h_low, h_high = zero, zero
            base = pl.multiple_of((x + 2) * 64, 64)
            for pair in range(NB // 2):
                both = g[x, 16 * pair : 16 * pair + 16, lanes(p)]
                both32 = both.astype(F32)
                ups, downs = [], []
                for half in range(2):
                    b = 2 * pair + half
                    v = both32[8 * half : 8 * half + 8]
                    ups.append(jnp.where(sub < 7, pltpu.roll(v, 7, 0), 0.0))
                    downs.append(jnp.where(sub > 0, pltpu.roll(v, 1, 0), 0.0))
                    h_low = jnp.where(sub == b, pltpu.roll(v, b, 0) if b else v, h_low)
                    h_high = jnp.where(sub == b, pltpu.roll(v, b + 1, 0), h_high)
                rows = pl.ds(pl.multiple_of(base + 16 * pair, 16), 16)
                gext[rows, cols[0] : cols[0] + 128] = jnp.concatenate(ups, 0).astype(BF16)
                gext[rows, cols[1] : cols[1] + 128] = both
                gext[rows, cols[2] : cols[2] + 128] = jnp.concatenate(downs, 0).astype(BF16)
            rows = pl.ds(pl.multiple_of(base + 48, 16), 16)
            gext[rows, cols[0] : cols[0] + 128] = jnp.concatenate([h_low, zero], 0).astype(BF16)
            gext[rows, cols[1] : cols[1] + 128] = jnp.zeros((16, 128), BF16)
            gext[rows, cols[2] : cols[2] + 128] = jnp.concatenate([zero, h_high], 0).astype(BF16)
        return carry

    lax.fori_loop(0, 8, fill_g, 0)
    for copy in copies:
        copy.wait()

    def windows(tiles):
        merged = [
            jnp.where(low, tiles[p + 1], tiles[(p + 4) % 5]) for p in range(4)
        ]
        return [v for p in range(4) for v in (tiles[p], merged[p])]

    def five(b, ox, oy, xs):
        def source(oz):
            if (ox, oy, oz) == (0, 0, 0):
                return table[b, xs].astype(F32)
            return table[nbr[b, SLOT_OF[ox, oy, oz]], xs].astype(F32)

        centre, after, before = source(0), source(1), source(-1)
        tiles = [centre[:, lanes(t)] for t in range(4)]
        return tiles + [jnp.where(low, after[:, lanes(0)], before[:, lanes(3)])]

    def fill_plane(xx, ox, xs):
        base = pl.multiple_of(xx * 64, 64)
        h_low, h_high = [zero] * 5, [zero] * 5
        for pair in range(NB // 2):
            wins = []
            for b in (2 * pair, 2 * pair + 1):
                wins.append(windows(five(b, ox, 0, xs)))
                v = five(b, ox, -1, xs)
                h_low = [
                    jnp.where(sub == b, pltpu.roll(v[t], b + 1, 0), h_low[t]) for t in range(5)
                ]
                v = five(b, ox, 1, xs)
                h_high = [
                    jnp.where(sub == b, pltpu.roll(v[t], b, 0) if b else v[t], h_high[t])
                    for t in range(5)
                ]
            rows = pl.ds(pl.multiple_of(base + 16 * pair, 16), 16)
            for n in range(8):
                px[rows, lanes(n)] = jnp.concatenate([wins[0][n], wins[1][n]], 0).astype(BF16)
        wins = [windows(h_low), windows(h_high)]
        rows = pl.ds(pl.multiple_of(base + 48, 16), 16)
        for n in range(8):
            px[rows, lanes(n)] = jnp.concatenate([wins[0][n], wins[1][n]], 0).astype(BF16)

    fill_plane(0, -1, 7)

    def middle_fill(x, carry):
        fill_plane(x + 1, 0, x)
        return carry

    lax.fori_loop(0, 8, middle_fill, 0)
    fill_plane(9, 1, 0)

    for p in range(4):
        right = jnp.concatenate(
            [
                gext[(2 - a) * 64 : (2 - a) * 64 + 640, p * 384 : p * 384 + 384]
                for a in range(3)
            ],
            axis=1,
        )
        part = dot(px[:, 256 * p : 256 * p + 256], right, 0, 0)
        if p == 0:
            dsc[...] = part
        else:
            dsc[...] += part
    low64 = lax.broadcasted_iota(jnp.int32, (64, 128), 1) < 64
    row_of = (192, 0, 64, 128)
    taps = [(a, c, e) for a in range(3) for c in range(3) for e in range(3)]

    def tap_parts(tap):
        a, c, e = tap
        col = a * 384 + c * 128
        first = dsc[row_of[e] : row_of[e] + 64, col : col + 128]
        second = dsc[row_of[e + 1] : row_of[e + 1] + 64, col : col + 128]
        return first, second

    for n in range(14):
        first, second = tap_parts(taps[2 * n])
        left = first + pltpu.roll(second, 64, 1)
        if 2 * n + 1 < 27:
            first, second = tap_parts(taps[2 * n + 1])
            right = second + pltpu.roll(first, 64, 1)
        else:
            right = jnp.zeros((64, 128), F32)
        dwp[64 * n : 64 * n + 64, :] = jnp.where(low64, left, right)
    dwp[896:1024, :] = jnp.zeros((128, 128), F32)


def conv_kernel(px, wp, live, out, wf, gsc):
    sub = lax.broadcasted_iota(jnp.int32, (8, 128), 0)
    for a in range(3):
        for c in range(3):
            for n, t in enumerate((1, 2, 3, 0)):
                row = a * 256 + n * 64
                wf[row : row + 64, lanes(c)] = wp[(a * 3 + c) * 4 + t]
    for p in range(4):
        left = jnp.concatenate(
            [px[64 * a : 64 * a + 512, 256 * p : 256 * p + 256] for a in range(3)], axis=1
        )
        gsc[p] = dot(left, wf[...], 1, 0)

    def finish(x, carry):
        base = pl.multiple_of(x * 64, 64)
        for p in range(4):
            lo_rows = gsc[p, pl.ds(pl.multiple_of(base + 48, 8), 8), lanes(0)]
            hi_rows = gsc[p, pl.ds(pl.multiple_of(base + 56, 8), 8), lanes(2)]
            for b in range(NB):
                rows = pl.ds(pl.multiple_of(base + 8 * b, 8), 8)
                v = [gsc[p, rows, lanes(c)] for c in range(3)]
                lo = pltpu.roll(lo_rows, (8 - b) % 8, 0) if b else lo_rows
                hi = pltpu.roll(hi_rows, 7 - b, 0)
                total = (
                    v[1]
                    + jnp.where(sub > 0, pltpu.roll(v[0], 1, 0), lo)
                    + jnp.where(sub < 7, pltpu.roll(v[2], 7, 0), hi)
                )
                on = live[b, x, :, lanes(p)].astype(F32)
                out[b, x, :, lanes(p)] = (total * on).astype(BF16)
        return carry

    lax.fori_loop(0, 8, finish, 0)


def final_kernel(rloc, a0, a1, a2, a3, live, send, out, acc):
    acc[...] = rloc[...]
    for k, src in enumerate((a0, a1, a2, a3)):
        for j in range(CAP):
            row = send[0, k, j]

            @pl.when(row < NB)
            def _(src=src, j=j, row=row):
                for x in range(8):
                    acc[row * 8 + x] += src[j, x].astype(F32)

    for x in range(8):
        for b in range(NB):
            out[b, x] = (acc[b * 8 + x] * live[b, x].astype(F32)).astype(BF16)


def sum_kernel(parts, out, *, scale):
    out[...] = jnp.broadcast_to(
        (jnp.sum(parts[...], axis=0) * scale)[None], out.shape
    )


def unpack_kernel(packed, out):
    for n in range(14):
        tile = packed[64 * n : 64 * n + 64, :]
        out[2 * n] = tile[:, 0:64]
        if 2 * n + 1 < 27:
            out[2 * n + 1] = pltpu.roll(tile, 64, 1)[:, 0:64]


VM = pl.BlockSpec(memory_space=pltpu.VMEM)
SM = pl.BlockSpec(memory_space=pltpu.SMEM)
ANY = pl.BlockSpec(memory_space=pl.ANY)
BLOCK = jax.ShapeDtypeStruct((NB, 8, 8, 512), BF16)
SEND = jax.ShapeDtypeStruct((CAP, 8, 8, 512), BF16)


def on_device(features, grad_out, occupancy, weight, neighbours, send_rows):
    w = weight.reshape(9, 3, 64, 64)
    none = jnp.zeros((9, 1, 64, 64), BF16)
    wp = jnp.concatenate(
        [jnp.concatenate([w, none], axis=1), jnp.concatenate([none, w], axis=1)], axis=3
    ).reshape(36, 64, 128)

    shown, g, live, *sends = pl.pallas_call(
        prep_kernel,
        out_shape=(BLOCK, jax.ShapeDtypeStruct((8, 48, 512), BF16), BLOCK, SEND, SEND, SEND, SEND),
        in_specs=[VM, VM, VM, SM],
        out_specs=[VM] * 7,
        scratch_shapes=[pltpu.VMEM((NB * 64, 512), F32)],
        name="prep",
    )(features, grad_out, occupancy, send_rows)
    with jax.named_scope("halo"):
        arrived = [shifted(s, "space", d) for s, d in zip(sends, DISTANCES)]
    rloc, *backs = pl.pallas_call(
        dgrad_kernel,
        out_shape=(jax.ShapeDtypeStruct((NB * 8, 8, 512), F32), SEND, SEND, SEND, SEND),
        in_specs=[VM, VM, SM],
        out_specs=[VM] * 5,
        scratch_shapes=[
            pltpu.VMEM((576, 768), BF16),
            pltpu.VMEM((384, 768), BF16),
            pltpu.VMEM((5, 480, 384), F32),
            pltpu.VMEM((NT * 8, 8, 512), F32),
        ],
        name="dgrad",
    )(g, wp, neighbours)
    px, dwp = pl.pallas_call(
        wgrad_kernel,
        out_shape=(jax.ShapeDtypeStruct((640, 1024), BF16), jax.ShapeDtypeStruct((1024, 128), F32)),
        in_specs=[ANY] * 6 + [VM, SM],
        out_specs=[VM] * 2,
        scratch_shapes=[
            pltpu.VMEM((NT, 8, 8, 512), BF16),
            pltpu.VMEM((768, 1536), BF16),
            pltpu.VMEM((256, 1152), F32),
            pltpu.SemaphoreType.DMA((5,)),
        ],
        name="wgrad",
    )(shown, *arrived, rloc, g, neighbours)
    output = pl.pallas_call(
        conv_kernel,
        out_shape=BLOCK,
        in_specs=[VM] * 3,
        out_specs=VM,
        scratch_shapes=[pltpu.VMEM((768, 384), BF16), pltpu.VMEM((4, 512, 384), F32)],
        name="conv",
    )(px, wp, live)
    *backs, dwp = lax.optimization_barrier((*backs, dwp))
    with jax.named_scope("back"):
        returned = [shifted(s, "space", -d) for s, d in zip(backs, DISTANCES)]

    count = lax.axis_size("space") * lax.axis_size("dp")
    scale = 1.0 / math.sqrt(count * NB * 512)
    axes = ("space", "dp")
    rows = 1024 // count
    with jax.named_scope("scatter"):
        parts = lax.all_to_all(dwp.reshape(count, rows, 128), axes, 0, 0, tiled=True)
    total = pl.pallas_call(
        lambda parts, out: sum_kernel(parts, out, scale=scale),
        out_shape=jax.ShapeDtypeStruct((count, rows, 128), F32),
        in_specs=[VM],
        out_specs=VM,
        name="sum",
    )(parts)
    with jax.named_scope("gather"):
        packed = lax.all_to_all(total, axes, 0, 0, tiled=True).reshape(1024, 128)
    weight_grad = pl.pallas_call(
        unpack_kernel,
        out_shape=jax.ShapeDtypeStruct((27, 64, 64), F32),
        in_specs=[VM],
        out_specs=VM,
        name="unpack",
    )(packed).reshape(3, 3, 3, 64, 64)
    feature_grad = pl.pallas_call(
        final_kernel,
        out_shape=BLOCK,
        in_specs=[VM] * 6 + [SM],
        out_specs=VM,
        scratch_shapes=[pltpu.VMEM((NB * 8, 8, 512), F32)],
        name="final",
    )(rloc, *returned, live, send_rows)
    return (output, feature_grad, weight_grad)


def solution(mesh):
    return jax.shard_map(
        on_device,
        mesh=mesh,
        in_specs=(
            P(("space", "dp"), None, None, None),
            P(("space", "dp"), None, None, None),
            P(("space", "dp"), None),
            P(),
            P(("space", "dp"), None),
            P(("space", "dp"), None, None),
        ),
        out_specs=(P(("space", "dp"), None, None, None), P(("space", "dp"), None, None, None), P()),
        check_vma=False,
    )
```

```python
import functools
import math

import jax
import jax.numpy as jnp
from jax import lax
from jax.experimental import pallas as pl
from jax.experimental.pallas import tpu as pltpu
from jax.sharding import PartitionSpec as P

DISTANCES = (1, -1, 2, -2)
OFFSETS = [
    (step_x, step_y, step_z)
    for step_x in (-1, 0, 1)
    for step_y in (-1, 0, 1)
    for step_z in (-1, 0, 1)
    if (step_x, step_y, step_z) != (0, 0, 0)
]
SLOT_OF = {offset: num for num, offset in enumerate(OFFSETS)}
BF16 = jnp.bfloat16
F32 = jnp.float32
NB = 6
CAP = 2
NT = NB + 4 * CAP + 1


def shifted(block, axis, distance):
    devices = range(lax.axis_size(axis))
    route = [(i - distance, i) for i in devices if i - distance in devices]
    return lax.ppermute(block, axis, route)


def first_hop(lists, sign):
    steps = (sign, -sign, sign, -sign)
    moved = [shifted(lists[k], "space", steps[k]) for k in (2, 3, 0, 1)]
    return [moved[2], moved[3], moved[0], moved[1]]


def second_hop(lists, sign):
    return [lists[0], lists[1], shifted(lists[2], "space", sign), shifted(lists[3], "space", -sign)]


def dot(left, right, left_dim, right_dim):
    dims = (((left_dim,), (right_dim,)), ((), ()))
    return lax.dot_general(left, right, dims, preferred_element_type=F32)


def live_block(occ_row):
    voxel = lax.broadcasted_iota(jnp.int32, (64, 512), 1)
    line = lax.broadcasted_iota(jnp.int32, (64, 512), 0)
    left = jnp.where(voxel // 8 == line, jnp.broadcast_to(occ_row, (64, 512)), 0)
    voxel = lax.broadcasted_iota(jnp.int32, (512, 512), 0)
    lane = lax.broadcasted_iota(jnp.int32, (512, 512), 1)
    spread = jnp.where(voxel % 8 == lane // 64, 1.0, 0.0)
    return dot(left.astype(F32).astype(BF16), spread.astype(BF16), 1, 0)


def lanes(t):
    return slice(128 * t, 128 * t + 128)


def prep_kernel(feat, grad, occ, send, shown, g, live, s0, s1, s2, s3, mask):
    for b in range(NB):
        mask[64 * b : 64 * b + 64, :] = live_block(occ[b : b + 1, :])
    for x in range(8):
        for pair in range(NB // 2):
            parts = []
            for b in (2 * pair, 2 * pair + 1):
                on = mask[b * 64 + x * 8 : b * 64 + x * 8 + 8, :]
                live[b, x] = on.astype(BF16)
                f = feat[b, x].astype(F32)
                shown[b, x] = jnp.where(on > 0.5, f, 0.0).astype(BF16)
                parts.append(jnp.where(on > 0.5, grad[b, x].astype(F32), 0.0))
            g[x, 16 * pair : 16 * pair + 16, :] = jnp.concatenate(parts, axis=0).astype(BF16)
    for k, out in enumerate((s0, s1, s2, s3)):
        for j in range(CAP):
            row = jnp.minimum(send[0, k, j], NB - 1)
            out[j] = shown[row]


def dgrad_kernel(g, wp, nbr, rloc, r0, r1, r2, r3, gext, wbt, dsc, acc):
    gext[0:96, :] = jnp.zeros((96, 768), BF16)
    gext[480:576, :] = jnp.zeros((96, 768), BF16)
    gext[96:480, 0:128] = jnp.zeros((384, 128), BF16)
    gext[96:480, 640:768] = jnp.zeros((384, 128), BF16)
    for x in range(8):
        gext[96 + 48 * x : 144 + 48 * x, 128:640] = g[x]
    for a in range(3):
        for c in range(3):
            for o in range(2):
                for s in range(2):
                    row = c * 128 + (1 - o) * 64
                    wbt[row : row + 64, a * 256 + s * 128 : a * 256 + s * 128 + 128] = wp[
                        (a * 3 + c) * 4 + o + 2 - 2 * s
                    ]
    for q in range(5):
        left = jnp.concatenate(
            [
                gext[(2 - a) * 48 : (2 - a) * 48 + 480, 128 * q : 128 * q + 256]
                for a in range(3)
            ],
            axis=1,
        )
        dsc[q] = dot(left, wbt[...], 1, 1)
    acc[...] = jnp.zeros((NT * 8, 8, 512), F32)
    low = lax.broadcasted_iota(jnp.int32, (8, 128), 1) < 64
    sub = lax.broadcasted_iota(jnp.int32, (8, 128), 0)

    def add_rows(b, offset, xs, tiles):
        def target(oz):
            if (offset[0], offset[1], oz) == (0, 0, 0):
                return b * 8 + xs
            return nbr[b, SLOT_OF[offset[0], offset[1], oz]] * 8 + xs

        row = target(0)
        for t in range(4):
            acc[row, :, lanes(t)] += tiles[t]
        row = target(1)
        acc[row, :, lanes(0)] += jnp.where(low, tiles[4], 0.0)
        row = target(-1)
        acc[row, :, lanes(3)] += jnp.where(low, 0.0, tiles[4])

    def group(xx, ox, xs):
        for b in range(NB):
            base = pl.multiple_of(xx * 48 + b * 8, 8)
            z = []
            for c in range(3):
                d = [dsc[t, pl.ds(base, 8), lanes(c)] for t in range(5)]
                z.append([jnp.where(low, d[t], d[(t + 1) % 5]) for t in range(5)])
            up = [pltpu.roll(v, 7, 0) for v in z[0]]
            down = [pltpu.roll(v, 1, 0) for v in z[2]]
            inner = [
                z[1][t] + jnp.where(sub < 7, up[t], 0.0) + jnp.where(sub > 0, down[t], 0.0)
                for t in range(5)
            ]
            add_rows(b, (ox, 0), xs, inner)
            add_rows(b, (ox, -1), xs, [jnp.where(sub == 7, v, 0.0) for v in up])
            add_rows(b, (ox, 1), xs, [jnp.where(sub == 0, v, 0.0) for v in down])

    group(0, -1, 7)

    def middle(x, carry):
        group(x + 1, 0, x)
        return carry

    lax.fori_loop(0, 8, middle, 0)
    group(9, 1, 0)
    rloc[...] = acc[0 : NB * 8]
    for k, out in enumerate((r0, r1, r2, r3)):
        for j in range(CAP):
            for x in range(8):
                out[j, x] = acc[(NB + CAP * k + j) * 8 + x].astype(BF16)


def wgrad_kernel(shown, a0, a1, a2, a3, after, g, nbr, px, dwp, table, gext, dsc, sems):
    copies = [pltpu.make_async_copy(shown, table.at[0:NB], sems.at[0])]
    for k, src in enumerate((a0, a1, a2, a3)):
        start = NB + CAP * k
        copies.append(
            pltpu.make_async_copy(src, table.at[start : start + CAP], sems.at[k + 1])
        )
    for copy in copies:
        copy.start()
    low = lax.broadcasted_iota(jnp.int32, (8, 128), 1) < 64
    sub = lax.broadcasted_iota(jnp.int32, (8, 128), 0)
    zero = jnp.zeros((8, 128), F32)
    table[NT - 1] = jnp.zeros((8, 8, 512), BF16)
    gext[0:128, :] = jnp.zeros((128, 1536), BF16)
    gext[640:768, :] = jnp.zeros((128, 1536), BF16)

    def fill_g(x, carry):
        for p in range(4):
            cols = [p * 384 + c * 128 for c in range(3)]
            h_low, h_high = zero, zero
            base = pl.multiple_of((x + 2) * 64, 64)
            for pair in range(NB // 2):
                both = g[x, 16 * pair : 16 * pair + 16, lanes(p)]
                both32 = both.astype(F32)
                ups, downs = [], []
                for half in range(2):
                    b = 2 * pair + half
                    v = both32[8 * half : 8 * half + 8]
                    ups.append(jnp.where(sub < 7, pltpu.roll(v, 7, 0), 0.0))
                    downs.append(jnp.where(sub > 0, pltpu.roll(v, 1, 0), 0.0))
                    h_low = jnp.where(sub == b, pltpu.roll(v, b, 0) if b else v, h_low)
                    h_high = jnp.where(sub == b, pltpu.roll(v, b + 1, 0), h_high)
                rows = pl.ds(pl.multiple_of(base + 16 * pair, 16), 16)
                gext[rows, cols[0] : cols[0] + 128] = jnp.concatenate(ups, 0).astype(BF16)
                gext[rows, cols[1] : cols[1] + 128] = both
                gext[rows, cols[2] : cols[2] + 128] = jnp.concatenate(downs, 0).astype(BF16)
            rows = pl.ds(pl.multiple_of(base + 48, 16), 16)
            gext[rows, cols[0] : cols[0] + 128] = jnp.concatenate([h_low, zero], 0).astype(BF16)
            gext[rows, cols[1] : cols[1] + 128] = jnp.zeros((16, 128), BF16)
            gext[rows, cols[2] : cols[2] + 128] = jnp.concatenate([zero, h_high], 0).astype(BF16)
        return carry

    lax.fori_loop(0, 8, fill_g, 0)
    for copy in copies:
        copy.wait()

    def windows(tiles):
        merged = [
            jnp.where(low, tiles[p + 1], tiles[(p + 4) % 5]) for p in range(4)
        ]
        return [v for p in range(4) for v in (tiles[p], merged[p])]

    def five(b, ox, oy, xs):
        def source(oz):
            if (ox, oy, oz) == (0, 0, 0):
                return table[b, xs].astype(F32)
            return table[nbr[b, SLOT_OF[ox, oy, oz]], xs].astype(F32)

        centre, after, before = source(0), source(1), source(-1)
        tiles = [centre[:, lanes(t)] for t in range(4)]
        return tiles + [jnp.where(low, after[:, lanes(0)], before[:, lanes(3)])]

    def fill_plane(xx, ox, xs):
        base = pl.multiple_of(xx * 64, 64)
        h_low, h_high = [zero] * 5, [zero] * 5
        for pair in range(NB // 2):
            wins = []
            for b in (2 * pair, 2 * pair + 1):
                wins.append(windows(five(b, ox, 0, xs)))
                v = five(b, ox, -1, xs)
                h_low = [
                    jnp.where(sub == b, pltpu.roll(v[t], b + 1, 0), h_low[t]) for t in range(5)
                ]
                v = five(b, ox, 1, xs)
                h_high = [
                    jnp.where(sub == b, pltpu.roll(v[t], b, 0) if b else v[t], h_high[t])
                    for t in range(5)
                ]
            rows = pl.ds(pl.multiple_of(base + 16 * pair, 16), 16)
            for n in range(8):
                px[rows, lanes(n)] = jnp.concatenate([wins[0][n], wins[1][n]], 0).astype(BF16)
        wins = [windows(h_low), windows(h_high)]
        rows = pl.ds(pl.multiple_of(base + 48, 16), 16)
        for n in range(8):
            px[rows, lanes(n)] = jnp.concatenate([wins[0][n], wins[1][n]], 0).astype(BF16)

    fill_plane(0, -1, 7)

    def middle_fill(x, carry):
        fill_plane(x + 1, 0, x)
        return carry

    lax.fori_loop(0, 8, middle_fill, 0)
    fill_plane(9, 1, 0)

    for p in range(4):
        right = jnp.concatenate(
            [
                gext[(2 - a) * 64 : (2 - a) * 64 + 640, p * 384 : p * 384 + 384]
                for a in range(3)
            ],
            axis=1,
        )
        part = dot(px[:, 256 * p : 256 * p + 256], right, 0, 0)
        if p == 0:
            dsc[...] = part
        else:
            dsc[...] += part
    low64 = lax.broadcasted_iota(jnp.int32, (64, 128), 1) < 64
    row_of = (192, 0, 64, 128)
    taps = [(a, c, e) for a in range(3) for c in range(3) for e in range(3)]

    def tap_parts(tap):
        a, c, e = tap
        col = a * 384 + c * 128
        first = dsc[row_of[e] : row_of[e] + 64, col : col + 128]
        second = dsc[row_of[e + 1] : row_of[e + 1] + 64, col : col + 128]
        return first, second

    for n in range(14):
        first, second = tap_parts(taps[2 * n])
        left = first + pltpu.roll(second, 64, 1)
        if 2 * n + 1 < 27:
            first, second = tap_parts(taps[2 * n + 1])
            right = second + pltpu.roll(first, 64, 1)
        else:
            right = jnp.zeros((64, 128), F32)
        dwp[64 * n : 64 * n + 64, :] = jnp.where(low64, left, right)
    dwp[896:1024, :] = jnp.zeros((128, 128), F32)


def conv_kernel(px, wp, live, out, wf, gsc):
    sub = lax.broadcasted_iota(jnp.int32, (8, 128), 0)
    for a in range(3):
        for c in range(3):
            for n, t in enumerate((1, 2, 3, 0)):
                row = a * 256 + n * 64
                wf[row : row + 64, lanes(c)] = wp[(a * 3 + c) * 4 + t]
    for p in range(4):
        left = jnp.concatenate(
            [px[64 * a : 64 * a + 512, 256 * p : 256 * p + 256] for a in range(3)], axis=1
        )
        gsc[p] = dot(left, wf[...], 1, 0)

    def finish(x, carry):
        base = pl.multiple_of(x * 64, 64)
        for p in range(4):
            lo_rows = gsc[p, pl.ds(pl.multiple_of(base + 48, 8), 8), lanes(0)]
            hi_rows = gsc[p, pl.ds(pl.multiple_of(base + 56, 8), 8), lanes(2)]
            for b in range(NB):
                rows = pl.ds(pl.multiple_of(base + 8 * b, 8), 8)
                v = [gsc[p, rows, lanes(c)] for c in range(3)]
                lo = pltpu.roll(lo_rows, (8 - b) % 8, 0) if b else lo_rows
                hi = pltpu.roll(hi_rows, 7 - b, 0)
                total = (
                    v[1]
                    + jnp.where(sub > 0, pltpu.roll(v[0], 1, 0), lo)
                    + jnp.where(sub < 7, pltpu.roll(v[2], 7, 0), hi)
                )
                on = live[b, x, :, lanes(p)].astype(F32)
                out[b, x, :, lanes(p)] = (total * on).astype(BF16)
        return carry

    lax.fori_loop(0, 8, finish, 0)


def final_kernel(rloc, a0, a1, a2, a3, live, send, out, acc):
    acc[...] = rloc[...]
    for k, src in enumerate((a0, a1, a2, a3)):
        for j in range(CAP):
            row = send[0, k, j]

            @pl.when(row < NB)
            def _(src=src, j=j, row=row):
                for x in range(8):
                    acc[row * 8 + x] += src[j, x].astype(F32)

    for x in range(8):
        for b in range(NB):
            out[b, x] = (acc[b * 8 + x] * live[b, x].astype(F32)).astype(BF16)


def sum_kernel(parts, *refs, scale):
    out = refs[-1]
    out[...] = jnp.broadcast_to(
        (jnp.sum(parts[...], axis=0) * scale)[None], out.shape
    )


def unpack_kernel(packed, out):
    for n in range(14):
        tile = packed[64 * n : 64 * n + 64, :]
        out[2 * n] = tile[:, 0:64]
        if 2 * n + 1 < 27:
            out[2 * n + 1] = pltpu.roll(tile, 64, 1)[:, 0:64]


VM = pl.BlockSpec(memory_space=pltpu.VMEM)
SM = pl.BlockSpec(memory_space=pltpu.SMEM)
ANY = pl.BlockSpec(memory_space=pl.ANY)
BLOCK = jax.ShapeDtypeStruct((NB, 8, 8, 512), BF16)
SEND = jax.ShapeDtypeStruct((CAP, 8, 8, 512), BF16)


def on_device(features, grad_out, occupancy, weight, neighbours, send_rows):
    w = weight.reshape(9, 3, 64, 64)
    none = jnp.zeros((9, 1, 64, 64), BF16)
    wp = jnp.concatenate(
        [jnp.concatenate([w, none], axis=1), jnp.concatenate([none, w], axis=1)], axis=3
    ).reshape(36, 64, 128)

    shown, g, live, *sends = pl.pallas_call(
        prep_kernel,
        out_shape=(BLOCK, jax.ShapeDtypeStruct((8, 48, 512), BF16), BLOCK, SEND, SEND, SEND, SEND),
        in_specs=[VM, VM, VM, SM],
        out_specs=[VM] * 7,
        scratch_shapes=[pltpu.VMEM((NB * 64, 512), F32)],
        name="prep",
    )(features, grad_out, occupancy, send_rows)
    with jax.named_scope("halo"):
        arrived = second_hop(first_hop(sends, 1), 1)
    rloc, *backs = pl.pallas_call(
        dgrad_kernel,
        out_shape=(jax.ShapeDtypeStruct((NB * 8, 8, 512), F32), SEND, SEND, SEND, SEND),
        in_specs=[VM, VM, SM],
        out_specs=[VM] * 5,
        scratch_shapes=[
            pltpu.VMEM((576, 768), BF16),
            pltpu.VMEM((384, 768), BF16),
            pltpu.VMEM((5, 480, 384), F32),
            pltpu.VMEM((NT * 8, 8, 512), F32),
        ],
        name="dgrad",
    )(g, wp, neighbours)
    px, dwp = pl.pallas_call(
        wgrad_kernel,
        out_shape=(jax.ShapeDtypeStruct((640, 1024), BF16), jax.ShapeDtypeStruct((1024, 128), F32)),
        in_specs=[ANY] * 6 + [VM, SM],
        out_specs=[VM] * 2,
        scratch_shapes=[
            pltpu.VMEM((NT, 8, 8, 512), BF16),
            pltpu.VMEM((768, 1536), BF16),
            pltpu.VMEM((256, 1152), F32),
            pltpu.SemaphoreType.DMA((5,)),
        ],
        name="wgrad",
    )(shown, *arrived, rloc, g, neighbours)
    output = pl.pallas_call(
        conv_kernel,
        out_shape=BLOCK,
        in_specs=[VM] * 3,
        out_specs=VM,
        scratch_shapes=[pltpu.VMEM((768, 384), BF16), pltpu.VMEM((4, 512, 384), F32)],
        name="conv",
    )(px, wp, live)
    *backs, output = lax.optimization_barrier((*backs, output))
    with jax.named_scope("back"):
        halfway = first_hop(backs, -1)

    count = lax.axis_size("space") * lax.axis_size("dp")
    scale = 1.0 / math.sqrt(count * NB * 512)
    axes = ("space", "dp")
    rows = 1024 // count
    with jax.named_scope("scatter"):
        parts = lax.all_to_all(dwp.reshape(count, rows, 128), axes, 0, 0, tiled=True)
    total = pl.pallas_call(
        functools.partial(sum_kernel, scale=scale),
        out_shape=jax.ShapeDtypeStruct((count, rows, 128), F32),
        in_specs=[VM] + [ANY] * 5,
        out_specs=VM,
        name="sum",
    )(parts, output, *halfway)
    total, halfway[2], halfway[3] = lax.optimization_barrier((total, halfway[2], halfway[3]))
    with jax.named_scope("back"):
        returned = second_hop(halfway, -1)
    with jax.named_scope("gather"):
        packed = lax.all_to_all(total, axes, 0, 0, tiled=True).reshape(1024, 128)
    weight_grad = pl.pallas_call(
        unpack_kernel,
        out_shape=jax.ShapeDtypeStruct((27, 64, 64), F32),
        in_specs=[VM],
        out_specs=VM,
        name="unpack",
    )(packed).reshape(3, 3, 3, 64, 64)
    feature_grad = pl.pallas_call(
        final_kernel,
        out_shape=BLOCK,
        in_specs=[VM] * 6 + [SM],
        out_specs=VM,
        scratch_shapes=[pltpu.VMEM((NB * 8, 8, 512), F32)],
        name="final",
    )(rloc, *returned, live, send_rows)
    return (output, feature_grad, weight_grad)


def solution(mesh):
    return jax.shard_map(
        on_device,
        mesh=mesh,
        in_specs=(
            P(("space", "dp"), None, None, None),
            P(("space", "dp"), None, None, None),
            P(("space", "dp"), None),
            P(),
            P(("space", "dp"), None),
            P(("space", "dp"), None, None),
        ),
        out_specs=(P(("space", "dp"), None, None, None), P(("space", "dp"), None, None, None), P()),
        check_vma=False,
    )
```

```python
import functools
import math

import jax
import jax.numpy as jnp
from jax import lax
from jax.experimental import pallas as pl
from jax.experimental.pallas import tpu as pltpu
from jax.sharding import Mesh
from jax.sharding import PartitionSpec as P

DISTANCES = (1, -1, 2, -2)
OFFSETS = [
    (step_x, step_y, step_z)
    for step_x in (-1, 0, 1)
    for step_y in (-1, 0, 1)
    for step_z in (-1, 0, 1)
    if (step_x, step_y, step_z) != (0, 0, 0)
]
SLOT_OF = {offset: num for num, offset in enumerate(OFFSETS)}
BF16 = jnp.bfloat16
F32 = jnp.float32
NB = 6
CAP = 2
NT = NB + 4 * CAP + 1


SPACE = ("y", "z", "x")
PLANE = ("y", "x", "dp")


def shifted(block, distance):
    devices = range(lax.axis_size(SPACE))
    route = [(i - distance, i) for i in devices if i - distance in devices]
    return lax.ppermute(block, SPACE, route)


def after(value, *others):
    return lax.optimization_barrier((value, *others))[0]


def dot(left, right, left_dim, right_dim):
    dims = (((left_dim,), (right_dim,)), ((), ()))
    return lax.dot_general(left, right, dims, preferred_element_type=F32)


def live_block(occ_row):
    voxel = lax.broadcasted_iota(jnp.int32, (64, 512), 1)
    line = lax.broadcasted_iota(jnp.int32, (64, 512), 0)
    left = jnp.where(voxel // 8 == line, jnp.broadcast_to(occ_row, (64, 512)), 0)
    voxel = lax.broadcasted_iota(jnp.int32, (512, 512), 0)
    lane = lax.broadcasted_iota(jnp.int32, (512, 512), 1)
    spread = jnp.where(voxel % 8 == lane // 64, 1.0, 0.0)
    return dot(left.astype(F32).astype(BF16), spread.astype(BF16), 1, 0)


def lanes(t):
    return slice(128 * t, 128 * t + 128)


def prep_kernel(feat, occ, send, shown, live, s0, s1, s2, s3, mask):
    for b in range(NB):
        mask[64 * b : 64 * b + 64, :] = live_block(occ[b : b + 1, :])
    for x in range(8):
        for b in range(NB):
            on = mask[b * 64 + x * 8 : b * 64 + x * 8 + 8, :]
            live[b, x] = on.astype(BF16)
            shown[b, x] = jnp.where(on > 0.5, feat[b, x].astype(F32), 0.0).astype(BF16)
    for k, out in enumerate((s0, s1, s2, s3)):
        for j in range(CAP):
            row = jnp.minimum(send[0, k, j], NB - 1)
            out[j] = shown[row]


def grad_kernel(grad, live, g):
    for x in range(8):
        for pair in range(NB // 2):
            parts = []
            for b in (2 * pair, 2 * pair + 1):
                on = live[b, x].astype(F32) > 0.5
                parts.append(jnp.where(on, grad[b, x].astype(F32), 0.0))
            g[x, 16 * pair : 16 * pair + 16, :] = jnp.concatenate(parts, axis=0).astype(BF16)


def dgrad_kernel(g, wp, nbr, rloc, r0, r1, r2, r3, gext, wbt, dsc, acc):
    gext[0:96, :] = jnp.zeros((96, 768), BF16)
    gext[480:576, :] = jnp.zeros((96, 768), BF16)
    gext[96:480, 0:128] = jnp.zeros((384, 128), BF16)
    gext[96:480, 640:768] = jnp.zeros((384, 128), BF16)
    for x in range(8):
        gext[96 + 48 * x : 144 + 48 * x, 128:640] = g[x]
    for a in range(3):
        for c in range(3):
            for o in range(2):
                for s in range(2):
                    row = c * 128 + (1 - o) * 64
                    wbt[row : row + 64, a * 256 + s * 128 : a * 256 + s * 128 + 128] = wp[
                        (a * 3 + c) * 4 + o + 2 - 2 * s
                    ]
    for q in range(5):
        left = jnp.concatenate(
            [
                gext[(2 - a) * 48 : (2 - a) * 48 + 480, 128 * q : 128 * q + 256]
                for a in range(3)
            ],
            axis=1,
        )
        dsc[q] = dot(left, wbt[...], 1, 1)
    acc[...] = jnp.zeros((NT * 8, 8, 512), F32)
    low = lax.broadcasted_iota(jnp.int32, (8, 128), 1) < 64
    sub = lax.broadcasted_iota(jnp.int32, (8, 128), 0)

    def add_rows(b, offset, xs, tiles):
        def target(oz):
            if (offset[0], offset[1], oz) == (0, 0, 0):
                return b * 8 + xs
            return nbr[b, SLOT_OF[offset[0], offset[1], oz]] * 8 + xs

        row = target(0)
        for t in range(4):
            acc[row, :, lanes(t)] += tiles[t]
        row = target(1)
        acc[row, :, lanes(0)] += jnp.where(low, tiles[4], 0.0)
        row = target(-1)
        acc[row, :, lanes(3)] += jnp.where(low, 0.0, tiles[4])

    def group(xx, ox, xs):
        for b in range(NB):
            base = pl.multiple_of(xx * 48 + b * 8, 8)
            z = []
            for c in range(3):
                d = [dsc[t, pl.ds(base, 8), lanes(c)] for t in range(5)]
                z.append([jnp.where(low, d[t], d[(t + 1) % 5]) for t in range(5)])
            up = [pltpu.roll(v, 7, 0) for v in z[0]]
            down = [pltpu.roll(v, 1, 0) for v in z[2]]
            inner = [
                z[1][t] + jnp.where(sub < 7, up[t], 0.0) + jnp.where(sub > 0, down[t], 0.0)
                for t in range(5)
            ]
            add_rows(b, (ox, 0), xs, inner)
            add_rows(b, (ox, -1), xs, [jnp.where(sub == 7, v, 0.0) for v in up])
            add_rows(b, (ox, 1), xs, [jnp.where(sub == 0, v, 0.0) for v in down])

    group(0, -1, 7)

    def middle(x, carry):
        group(x + 1, 0, x)
        return carry

    lax.fori_loop(0, 8, middle, 0)
    group(9, 1, 0)
    rloc[...] = acc[0 : NB * 8]
    for k, out in enumerate((r0, r1, r2, r3)):
        for j in range(CAP):
            for x in range(8):
                out[j, x] = acc[(NB + CAP * k + j) * 8 + x].astype(BF16)


def widen_kernel(g, gext):
    sub = lax.broadcasted_iota(jnp.int32, (8, 128), 0)
    zero = jnp.zeros((8, 128), F32)
    gext[0:128, :] = jnp.zeros((128, 1536), BF16)
    gext[640:768, :] = jnp.zeros((128, 1536), BF16)

    def fill_g(x, carry):
        for p in range(4):
            cols = [p * 384 + c * 128 for c in range(3)]
            h_low, h_high = zero, zero
            base = pl.multiple_of((x + 2) * 64, 64)
            for pair in range(NB // 2):
                both = g[x, 16 * pair : 16 * pair + 16, lanes(p)]
                both32 = both.astype(F32)
                ups, downs = [], []
                for half in range(2):
                    b = 2 * pair + half
                    v = both32[8 * half : 8 * half + 8]
                    ups.append(jnp.where(sub < 7, pltpu.roll(v, 7, 0), 0.0))
                    downs.append(jnp.where(sub > 0, pltpu.roll(v, 1, 0), 0.0))
                    h_low = jnp.where(sub == b, pltpu.roll(v, b, 0) if b else v, h_low)
                    h_high = jnp.where(sub == b, pltpu.roll(v, b + 1, 0), h_high)
                rows = pl.ds(pl.multiple_of(base + 16 * pair, 16), 16)
                gext[rows, cols[0] : cols[0] + 128] = jnp.concatenate(ups, 0).astype(BF16)
                gext[rows, cols[1] : cols[1] + 128] = both
                gext[rows, cols[2] : cols[2] + 128] = jnp.concatenate(downs, 0).astype(BF16)
            rows = pl.ds(pl.multiple_of(base + 48, 16), 16)
            gext[rows, cols[0] : cols[0] + 128] = jnp.concatenate([h_low, zero], 0).astype(BF16)
            gext[rows, cols[1] : cols[1] + 128] = jnp.zeros((16, 128), BF16)
            gext[rows, cols[2] : cols[2] + 128] = jnp.concatenate([zero, h_high], 0).astype(BF16)
        return carry

    lax.fori_loop(0, 8, fill_g, 0)


def wgrad_kernel(shown, a0, a1, a2, a3, before, gext, nbr, px, dwp, table, dsc, sems):
    copies = [pltpu.make_async_copy(shown, table.at[0:NB], sems.at[0])]
    for k, src in enumerate((a0, a1, a2, a3)):
        start = NB + CAP * k
        copies.append(
            pltpu.make_async_copy(src, table.at[start : start + CAP], sems.at[k + 1])
        )
    for copy in copies:
        copy.start()
    low = lax.broadcasted_iota(jnp.int32, (8, 128), 1) < 64
    sub = lax.broadcasted_iota(jnp.int32, (8, 128), 0)
    zero = jnp.zeros((8, 128), F32)
    table[NT - 1] = jnp.zeros((8, 8, 512), BF16)
    for copy in copies:
        copy.wait()

    def windows(tiles):
        merged = [
            jnp.where(low, tiles[p + 1], tiles[(p + 4) % 5]) for p in range(4)
        ]
        return [v for p in range(4) for v in (tiles[p], merged[p])]

    def five(b, ox, oy, xs):
        def source(oz):
            if (ox, oy, oz) == (0, 0, 0):
                return table[b, xs].astype(F32)
            return table[nbr[b, SLOT_OF[ox, oy, oz]], xs].astype(F32)

        centre, after, before = source(0), source(1), source(-1)
        tiles = [centre[:, lanes(t)] for t in range(4)]
        return tiles + [jnp.where(low, after[:, lanes(0)], before[:, lanes(3)])]

    def fill_plane(xx, ox, xs):
        base = pl.multiple_of(xx * 64, 64)
        h_low, h_high = [zero] * 5, [zero] * 5
        for pair in range(NB // 2):
            wins = []
            for b in (2 * pair, 2 * pair + 1):
                wins.append(windows(five(b, ox, 0, xs)))
                v = five(b, ox, -1, xs)
                h_low = [
                    jnp.where(sub == b, pltpu.roll(v[t], b + 1, 0), h_low[t]) for t in range(5)
                ]
                v = five(b, ox, 1, xs)
                h_high = [
                    jnp.where(sub == b, pltpu.roll(v[t], b, 0) if b else v[t], h_high[t])
                    for t in range(5)
                ]
            rows = pl.ds(pl.multiple_of(base + 16 * pair, 16), 16)
            for n in range(8):
                px[rows, lanes(n)] = jnp.concatenate([wins[0][n], wins[1][n]], 0).astype(BF16)
        wins = [windows(h_low), windows(h_high)]
        rows = pl.ds(pl.multiple_of(base + 48, 16), 16)
        for n in range(8):
            px[rows, lanes(n)] = jnp.concatenate([wins[0][n], wins[1][n]], 0).astype(BF16)

    fill_plane(0, -1, 7)

    def middle_fill(x, carry):
        fill_plane(x + 1, 0, x)
        return carry

    lax.fori_loop(0, 8, middle_fill, 0)
    fill_plane(9, 1, 0)

    for p in range(4):
        right = jnp.concatenate(
            [
                gext[(2 - a) * 64 : (2 - a) * 64 + 640, p * 384 : p * 384 + 384]
                for a in range(3)
            ],
            axis=1,
        )
        part = dot(px[:, 256 * p : 256 * p + 256], right, 0, 0)
        if p == 0:
            dsc[...] = part
        else:
            dsc[...] += part
    low64 = lax.broadcasted_iota(jnp.int32, (64, 128), 1) < 64
    row_of = (192, 0, 64, 128)
    taps = [(a, c, e) for a in range(3) for c in range(3) for e in range(3)]

    def tap_parts(tap):
        a, c, e = tap
        col = a * 384 + c * 128
        first = dsc[row_of[e] : row_of[e] + 64, col : col + 128]
        second = dsc[row_of[e + 1] : row_of[e + 1] + 64, col : col + 128]
        return first, second

    for n in range(14):
        first, second = tap_parts(taps[2 * n])
        left = first + pltpu.roll(second, 64, 1)
        if 2 * n + 1 < 27:
            first, second = tap_parts(taps[2 * n + 1])
            right = second + pltpu.roll(first, 64, 1)
        else:
            right = jnp.zeros((64, 128), F32)
        dwp[64 * n : 64 * n + 64, :] = jnp.where(low64, left, right)
    dwp[896:1024, :] = jnp.zeros((128, 128), F32)


def conv_kernel(px, wp, live, out, wf, gsc):
    sub = lax.broadcasted_iota(jnp.int32, (8, 128), 0)
    for a in range(3):
        for c in range(3):
            for n, t in enumerate((1, 2, 3, 0)):
                row = a * 256 + n * 64
                wf[row : row + 64, lanes(c)] = wp[(a * 3 + c) * 4 + t]
    for p in range(4):
        left = jnp.concatenate(
            [px[64 * a : 64 * a + 512, 256 * p : 256 * p + 256] for a in range(3)], axis=1
        )
        gsc[p] = dot(left, wf[...], 1, 0)

    def finish(x, carry):
        base = pl.multiple_of(x * 64, 64)
        for p in range(4):
            lo_rows = gsc[p, pl.ds(pl.multiple_of(base + 48, 8), 8), lanes(0)]
            hi_rows = gsc[p, pl.ds(pl.multiple_of(base + 56, 8), 8), lanes(2)]
            for b in range(NB):
                rows = pl.ds(pl.multiple_of(base + 8 * b, 8), 8)
                v = [gsc[p, rows, lanes(c)] for c in range(3)]
                lo = pltpu.roll(lo_rows, (8 - b) % 8, 0) if b else lo_rows
                hi = pltpu.roll(hi_rows, 7 - b, 0)
                total = (
                    v[1]
                    + jnp.where(sub > 0, pltpu.roll(v[0], 1, 0), lo)
                    + jnp.where(sub < 7, pltpu.roll(v[2], 7, 0), hi)
                )
                on = live[b, x, :, lanes(p)].astype(F32)
                out[b, x, :, lanes(p)] = (total * on).astype(BF16)
        return carry

    lax.fori_loop(0, 8, finish, 0)


def final_kernel(rloc, a0, a1, a2, a3, live, send, out, acc):
    acc[...] = rloc[...]
    for k, src in enumerate((a0, a1, a2, a3)):
        for j in range(CAP):
            row = send[0, k, j]

            @pl.when(row < NB)
            def _(src=src, j=j, row=row):
                for x in range(8):
                    acc[row * 8 + x] += src[j, x].astype(F32)

    for x in range(8):
        for b in range(NB):
            out[b, x] = (acc[b * 8 + x] * live[b, x].astype(F32)).astype(BF16)


def sum_kernel(parts, *refs, scale):
    out = refs[-1]
    total = parts[0]
    for n in range(1, parts.shape[0]):
        total = total + parts[n]
    total = total * scale
    for n in range(out.shape[0]):
        out[n] = total


def unpack_kernel(packed, out):
    for n in range(14):
        tile = packed[64 * n : 64 * n + 64, :]
        out[2 * n] = tile[:, 0:64]
        if 2 * n + 1 < 27:
            out[2 * n + 1] = pltpu.roll(tile, 64, 1)[:, 0:64]


def in_vmem(x):
    return pltpu.with_memory_space_constraint(x, pltpu.VMEM)


VM = pl.BlockSpec(memory_space=pltpu.VMEM)
SM = pl.BlockSpec(memory_space=pltpu.SMEM)
ANY = pl.BlockSpec(memory_space=pl.ANY)
BLOCK = jax.ShapeDtypeStruct((NB, 8, 8, 512), BF16)
SEND = jax.ShapeDtypeStruct((CAP, 8, 8, 512), BF16)


def call(kernel, name, ins, outs, scratch=(), **params):
    return pl.pallas_call(
        kernel,
        out_shape=outs,
        in_specs=ins,
        out_specs=jax.tree.map(lambda _: VM, outs),
        scratch_shapes=list(scratch),
        name=name,
        **params,
    )


def reduced(parts, copies, scale, name, *before):
    rows = parts.shape[1]
    out = jax.ShapeDtypeStruct((copies, rows, 128), F32)
    kernel = functools.partial(sum_kernel, scale=scale)
    return call(kernel, name, [VM] + [ANY] * len(before), out)(in_vmem(parts), *before)


def on_device(features, grad_out, occupancy, weight, neighbours, send_rows):
    shape = jax.ShapeDtypeStruct
    shown, live, *sends = call(
        prep_kernel,
        "prep",
        [VM, VM, SM],
        (BLOCK, BLOCK, SEND, SEND, SEND, SEND),
        [pltpu.VMEM((NB * 64, 512), F32)],
    )(features, occupancy, send_rows)
    arrived = [shifted(sends[0], 1)]
    g = call(grad_kernel, "grad", [VM, VM], shape((8, 48, 512), BF16))(grad_out, live)
    arrived.append(shifted(after(sends[1], g), -1))
    w = after(weight, g).reshape(9, 3, 64, 64)
    none = jnp.zeros((9, 1, 64, 64), BF16)
    wp = jnp.concatenate(
        [jnp.concatenate([w, none], axis=1), jnp.concatenate([none, w], axis=1)], axis=3
    ).reshape(36, 64, 128)
    arrived.append(shifted(after(sends[2], wp), 2))
    gext = call(widen_kernel, "widen", [VM], shape((768, 1536), BF16))(after(g, wp))
    arrived.append(shifted(after(sends[3], gext), -2))
    rloc, *backs = call(
        dgrad_kernel,
        "dgrad",
        [VM, VM, SM],
        (shape((NB * 8, 8, 512), F32), SEND, SEND, SEND, SEND),
        [
            pltpu.VMEM((576, 768), BF16),
            pltpu.VMEM((384, 768), BF16),
            pltpu.VMEM((5, 480, 384), F32),
            pltpu.VMEM((NT * 8, 8, 512), F32),
        ],
    )(after(g, gext), wp, neighbours)
    px, dwp = call(
        wgrad_kernel,
        "wgrad",
        [ANY, VM, VM, VM, VM, ANY, VM, SM],
        (shape((640, 1024), BF16), shape((1024, 128), F32)),
        [
            pltpu.VMEM((NT, 8, 8, 512), BF16),
            pltpu.VMEM((256, 1152), F32),
            pltpu.SemaphoreType.DMA((5,)),
        ],
    )(shown, *map(in_vmem, arrived), rloc, gext, neighbours)
    output = call(
        conv_kernel,
        "conv",
        [VM] * 3,
        BLOCK,
        [pltpu.VMEM((768, 384), BF16), pltpu.VMEM((4, 512, 384), F32)],
    )(px, wp, live)

    count = lax.axis_size(SPACE) * lax.axis_size("dp")
    scale = 1.0 / math.sqrt(count * NB * 512)
    near = lax.axis_size(PLANE)
    far = count // near
    rows = 1024 // near
    with jax.named_scope("scatter"):
        parts = lax.all_to_all(dwp.reshape(near, rows, 128), PLANE, 0, 0, tiled=True)
    total = reduced(parts, far, 1.0, "near_sum", output)
    with jax.named_scope("swap"):
        parts = lax.all_to_all(total, "z", 0, 0, tiled=True)
    backs = [after(back, total) for back in backs]
    returned = [shifted(backs[0], -1), shifted(backs[1], 1)]
    total = reduced(parts, near, scale, "far_sum", *map(lambda r: r, returned))
    with jax.named_scope("gather"):
        packed = lax.all_to_all(total, PLANE, 0, 0, tiled=True).reshape(1024, 128)
    returned.append(shifted(after(backs[2], total), -2))
    returned.append(shifted(after(backs[3], total), 2))
    weight_grad = call(unpack_kernel, "unpack", [VM], shape((27, 64, 64), F32))(in_vmem(packed))
    feature_grad = call(
        final_kernel,
        "final",
        [VM] * 6 + [SM],
        BLOCK,
        [pltpu.VMEM((NB * 8, 8, 512), F32)],
    )(rloc, *map(in_vmem, returned), live, send_rows)
    return (output, feature_grad, weight_grad.reshape(3, 3, 3, 64, 64))


def solution(mesh):
    grid = Mesh(mesh.devices.reshape(4, -1, 4, 2), ("y", "z", "x", "dp"))
    every = ("y", "z", "x", "dp")
    return jax.shard_map(
        on_device,
        mesh=grid,
        in_specs=(
            P(every, None, None, None),
            P(every, None, None, None),
            P(every, None),
            P(),
            P(every, None),
            P(every, None, None),
        ),
        out_specs=(P(every, None, None, None), P(every, None, None, None), P()),
        check_vma=False,
    )
```

```python
import functools
import math

import jax
import jax.numpy as jnp
from jax import lax
from jax.experimental import pallas as pl
from jax.experimental.pallas import tpu as pltpu
from jax.sharding import Mesh
from jax.sharding import PartitionSpec as P

STEPS = (1, 1, 2, 2)
FIRST = (0, 1, 0, 1)
OFFSETS = [
    (step_x, step_y, step_z)
    for step_x in (-1, 0, 1)
    for step_y in (-1, 0, 1)
    for step_z in (-1, 0, 1)
    if (step_x, step_y, step_z) != (0, 0, 0)
]
SLOT_OF = {offset: num for num, offset in enumerate(OFFSETS)}
BF16 = jnp.bfloat16
F32 = jnp.float32
NB = 6
CAP = 2
NT = NB + 4 * CAP + 1


SPACE = ("y", "z", "x")
PLANE = ("y", "x", "dp")


def swapped(block, step, first):
    count = lax.axis_size(SPACE)
    route = []
    for i in range(count):
        peer = i + step if (i // step) % 2 == first else i - step
        if 0 <= peer < count:
            route.append((i, peer))
    return lax.ppermute(block, SPACE, route)


def after(value, *others):
    return lax.optimization_barrier((value, *others))[0]


def dot(left, right, left_dim, right_dim):
    dims = (((left_dim,), (right_dim,)), ((), ()))
    return lax.dot_general(left, right, dims, preferred_element_type=F32)


def live_block(occ_row):
    voxel = lax.broadcasted_iota(jnp.int32, (64, 512), 1)
    line = lax.broadcasted_iota(jnp.int32, (64, 512), 0)
    left = jnp.where(voxel // 8 == line, jnp.broadcast_to(occ_row, (64, 512)), 0)
    voxel = lax.broadcasted_iota(jnp.int32, (512, 512), 0)
    lane = lax.broadcasted_iota(jnp.int32, (512, 512), 1)
    spread = jnp.where(voxel % 8 == lane // 64, 1.0, 0.0)
    return dot(left.astype(F32).astype(BF16), spread.astype(BF16), 1, 0)


def lanes(t):
    return slice(128 * t, 128 * t + 128)


def outgoing(column):
    low = column[0] & 1
    high = column[0] >> 1
    return (low, 1 - low, 2 + high, 3 - high)


def incoming(column):
    low, other, high, last = outgoing(column)
    return (1 - low, 1 - other, 5 - high, 5 - last)


def prep_kernel(feat, occ, send, column, shown, live, s0, s1, s2, s3, mask):
    for b in range(NB):
        mask[64 * b : 64 * b + 64, :] = live_block(occ[b : b + 1, :])
    for x in range(8):
        for b in range(NB):
            on = mask[b * 64 + x * 8 : b * 64 + x * 8 + 8, :]
            live[b, x] = on.astype(BF16)
            shown[b, x] = jnp.where(on > 0.5, feat[b, x].astype(F32), 0.0).astype(BF16)
    lists = outgoing(column)
    for n, out in enumerate((s0, s1, s2, s3)):
        for j in range(CAP):
            row = jnp.minimum(send[0, j, lists[n]], NB - 1)
            out[j] = shown[row]


def grad_kernel(grad, live, g):
    for x in range(8):
        for pair in range(NB // 2):
            parts = []
            for b in (2 * pair, 2 * pair + 1):
                on = live[b, x].astype(F32) > 0.5
                parts.append(jnp.where(on, grad[b, x].astype(F32), 0.0))
            g[x, 16 * pair : 16 * pair + 16, :] = jnp.concatenate(parts, axis=0).astype(BF16)


def dgrad_kernel(g, wp, nbr, column, rloc, r0, r1, r2, r3, gext, wbt, dsc, acc):
    gext[0:96, :] = jnp.zeros((96, 768), BF16)
    gext[480:576, :] = jnp.zeros((96, 768), BF16)
    gext[96:480, 0:128] = jnp.zeros((384, 128), BF16)
    gext[96:480, 640:768] = jnp.zeros((384, 128), BF16)
    for x in range(8):
        gext[96 + 48 * x : 144 + 48 * x, 128:640] = g[x]
    for a in range(3):
        for c in range(3):
            for o in range(2):
                for s in range(2):
                    row = c * 128 + (1 - o) * 64
                    wbt[row : row + 64, a * 256 + s * 128 : a * 256 + s * 128 + 128] = wp[
                        (a * 3 + c) * 4 + o + 2 - 2 * s
                    ]
    for q in range(5):
        left = jnp.concatenate(
            [
                gext[(2 - a) * 48 : (2 - a) * 48 + 480, 128 * q : 128 * q + 256]
                for a in range(3)
            ],
            axis=1,
        )
        dsc[q] = dot(left, wbt[...], 1, 1)
    acc[...] = jnp.zeros((NT * 8, 8, 512), F32)
    low = lax.broadcasted_iota(jnp.int32, (8, 128), 1) < 64
    sub = lax.broadcasted_iota(jnp.int32, (8, 128), 0)

    def add_rows(b, offset, xs, tiles):
        def target(oz):
            if (offset[0], offset[1], oz) == (0, 0, 0):
                return b * 8 + xs
            return nbr[b, SLOT_OF[offset[0], offset[1], oz]] * 8 + xs

        row = target(0)
        for t in range(4):
            acc[row, :, lanes(t)] += tiles[t]
        row = target(1)
        acc[row, :, lanes(0)] += jnp.where(low, tiles[4], 0.0)
        row = target(-1)
        acc[row, :, lanes(3)] += jnp.where(low, 0.0, tiles[4])

    def group(xx, ox, xs):
        for b in range(NB):
            base = pl.multiple_of(xx * 48 + b * 8, 8)
            z = []
            for c in range(3):
                d = [dsc[t, pl.ds(base, 8), lanes(c)] for t in range(5)]
                z.append([jnp.where(low, d[t], d[(t + 1) % 5]) for t in range(5)])
            up = [pltpu.roll(v, 7, 0) for v in z[0]]
            down = [pltpu.roll(v, 1, 0) for v in z[2]]
            inner = [
                z[1][t] + jnp.where(sub < 7, up[t], 0.0) + jnp.where(sub > 0, down[t], 0.0)
                for t in range(5)
            ]
            add_rows(b, (ox, 0), xs, inner)
            add_rows(b, (ox, -1), xs, [jnp.where(sub == 7, v, 0.0) for v in up])
            add_rows(b, (ox, 1), xs, [jnp.where(sub == 0, v, 0.0) for v in down])

    group(0, -1, 7)

    def middle(x, carry):
        group(x + 1, 0, x)
        return carry

    lax.fori_loop(0, 8, middle, 0)
    group(9, 1, 0)
    rloc[...] = acc[0 : NB * 8]
    lists = incoming(column)
    for n, out in enumerate((r0, r1, r2, r3)):
        start = NB + CAP * lists[n]
        for j in range(CAP):
            for x in range(8):
                out[j, x] = acc[(start + j) * 8 + x].astype(BF16)


def widen_kernel(g, gext):
    sub = lax.broadcasted_iota(jnp.int32, (8, 128), 0)
    zero = jnp.zeros((8, 128), F32)
    gext[0:128, :] = jnp.zeros((128, 1536), BF16)
    gext[640:768, :] = jnp.zeros((128, 1536), BF16)

    def fill_g(x, carry):
        for p in range(4):
            cols = [p * 384 + c * 128 for c in range(3)]
            h_low, h_high = zero, zero
            base = pl.multiple_of((x + 2) * 64, 64)
            for pair in range(NB // 2):
                both = g[x, 16 * pair : 16 * pair + 16, lanes(p)]
                both32 = both.astype(F32)
                ups, downs = [], []
                for half in range(2):
                    b = 2 * pair + half
                    v = both32[8 * half : 8 * half + 8]
                    ups.append(jnp.where(sub < 7, pltpu.roll(v, 7, 0), 0.0))
                    downs.append(jnp.where(sub > 0, pltpu.roll(v, 1, 0), 0.0))
                    h_low = jnp.where(sub == b, pltpu.roll(v, b, 0) if b else v, h_low)
                    h_high = jnp.where(sub == b, pltpu.roll(v, b + 1, 0), h_high)
                rows = pl.ds(pl.multiple_of(base + 16 * pair, 16), 16)
                gext[rows, cols[0] : cols[0] + 128] = jnp.concatenate(ups, 0).astype(BF16)
                gext[rows, cols[1] : cols[1] + 128] = both
                gext[rows, cols[2] : cols[2] + 128] = jnp.concatenate(downs, 0).astype(BF16)
            rows = pl.ds(pl.multiple_of(base + 48, 16), 16)
            gext[rows, cols[0] : cols[0] + 128] = jnp.concatenate([h_low, zero], 0).astype(BF16)
            gext[rows, cols[1] : cols[1] + 128] = jnp.zeros((16, 128), BF16)
            gext[rows, cols[2] : cols[2] + 128] = jnp.concatenate([zero, h_high], 0).astype(BF16)
        return carry

    lax.fori_loop(0, 8, fill_g, 0)


def wgrad_kernel(shown, a0, a1, a2, a3, before, gext, nbr, column, px, dwp, table, dsc, sems):
    copies = [pltpu.make_async_copy(shown, table.at[0:NB], sems.at[0])]
    lists = incoming(column)
    for n, src in enumerate((a0, a1, a2, a3)):
        start = NB + CAP * lists[n]
        copies.append(pltpu.make_async_copy(src, table.at[pl.ds(start, CAP)], sems.at[n + 1]))
    for copy in copies:
        copy.start()
    low = lax.broadcasted_iota(jnp.int32, (8, 128), 1) < 64
    sub = lax.broadcasted_iota(jnp.int32, (8, 128), 0)
    zero = jnp.zeros((8, 128), F32)
    table[NT - 1] = jnp.zeros((8, 8, 512), BF16)
    for copy in copies:
        copy.wait()

    def windows(tiles):
        merged = [
            jnp.where(low, tiles[p + 1], tiles[(p + 4) % 5]) for p in range(4)
        ]
        return [v for p in range(4) for v in (tiles[p], merged[p])]

    def five(b, ox, oy, xs):
        def source(oz):
            if (ox, oy, oz) == (0, 0, 0):
                return table[b, xs].astype(F32)
            return table[nbr[b, SLOT_OF[ox, oy, oz]], xs].astype(F32)

        centre, after, before = source(0), source(1), source(-1)
        tiles = [centre[:, lanes(t)] for t in range(4)]
        return tiles + [jnp.where(low, after[:, lanes(0)], before[:, lanes(3)])]

    def fill_plane(xx, ox, xs):
        base = pl.multiple_of(xx * 64, 64)
        h_low, h_high = [zero] * 5, [zero] * 5
        for pair in range(NB // 2):
            wins = []
            for b in (2 * pair, 2 * pair + 1):
                wins.append(windows(five(b, ox, 0, xs)))
                v = five(b, ox, -1, xs)
                h_low = [
                    jnp.where(sub == b, pltpu.roll(v[t], b + 1, 0), h_low[t]) for t in range(5)
                ]
                v = five(b, ox, 1, xs)
                h_high = [
                    jnp.where(sub == b, pltpu.roll(v[t], b, 0) if b else v[t], h_high[t])
                    for t in range(5)
                ]
            rows = pl.ds(pl.multiple_of(base + 16 * pair, 16), 16)
            for n in range(8):
                px[rows, lanes(n)] = jnp.concatenate([wins[0][n], wins[1][n]], 0).astype(BF16)
        wins = [windows(h_low), windows(h_high)]
        rows = pl.ds(pl.multiple_of(base + 48, 16), 16)
        for n in range(8):
            px[rows, lanes(n)] = jnp.concatenate([wins[0][n], wins[1][n]], 0).astype(BF16)

    fill_plane(0, -1, 7)

    def middle_fill(x, carry):
        fill_plane(x + 1, 0, x)
        return carry

    lax.fori_loop(0, 8, middle_fill, 0)
    fill_plane(9, 1, 0)

    for p in range(4):
        right = jnp.concatenate(
            [
                gext[(2 - a) * 64 : (2 - a) * 64 + 640, p * 384 : p * 384 + 384]
                for a in range(3)
            ],
            axis=1,
        )
        part = dot(px[:, 256 * p : 256 * p + 256], right, 0, 0)
        if p == 0:
            dsc[...] = part
        else:
            dsc[...] += part
    low64 = lax.broadcasted_iota(jnp.int32, (64, 128), 1) < 64
    row_of = (192, 0, 64, 128)
    taps = [(a, c, e) for a in range(3) for c in range(3) for e in range(3)]

    def tap_parts(tap):
        a, c, e = tap
        col = a * 384 + c * 128
        first = dsc[row_of[e] : row_of[e] + 64, col : col + 128]
        second = dsc[row_of[e + 1] : row_of[e + 1] + 64, col : col + 128]
        return first, second

    for n in range(14):
        first, second = tap_parts(taps[2 * n])
        left = first + pltpu.roll(second, 64, 1)
        if 2 * n + 1 < 27:
            first, second = tap_parts(taps[2 * n + 1])
            right = second + pltpu.roll(first, 64, 1)
        else:
            right = jnp.zeros((64, 128), F32)
        dwp[64 * n : 64 * n + 64, :] = jnp.where(low64, left, right)
    dwp[896:1024, :] = jnp.zeros((128, 128), F32)


def conv_kernel(px, wp, live, out, wf, gsc):
    sub = lax.broadcasted_iota(jnp.int32, (8, 128), 0)
    for a in range(3):
        for c in range(3):
            for n, t in enumerate((1, 2, 3, 0)):
                row = a * 256 + n * 64
                wf[row : row + 64, lanes(c)] = wp[(a * 3 + c) * 4 + t]
    for p in range(4):
        left = jnp.concatenate(
            [px[64 * a : 64 * a + 512, 256 * p : 256 * p + 256] for a in range(3)], axis=1
        )
        gsc[p] = dot(left, wf[...], 1, 0)

    def finish(x, carry):
        base = pl.multiple_of(x * 64, 64)
        for p in range(4):
            lo_rows = gsc[p, pl.ds(pl.multiple_of(base + 48, 8), 8), lanes(0)]
            hi_rows = gsc[p, pl.ds(pl.multiple_of(base + 56, 8), 8), lanes(2)]
            for b in range(NB):
                rows = pl.ds(pl.multiple_of(base + 8 * b, 8), 8)
                v = [gsc[p, rows, lanes(c)] for c in range(3)]
                lo = pltpu.roll(lo_rows, (8 - b) % 8, 0) if b else lo_rows
                hi = pltpu.roll(hi_rows, 7 - b, 0)
                total = (
                    v[1]
                    + jnp.where(sub > 0, pltpu.roll(v[0], 1, 0), lo)
                    + jnp.where(sub < 7, pltpu.roll(v[2], 7, 0), hi)
                )
                on = live[b, x, :, lanes(p)].astype(F32)
                out[b, x, :, lanes(p)] = (total * on).astype(BF16)
        return carry

    lax.fori_loop(0, 8, finish, 0)


def final_kernel(rloc, a0, a1, a2, a3, live, send, column, out, acc):
    acc[...] = rloc[...]
    lists = outgoing(column)
    for n, src in enumerate((a0, a1, a2, a3)):
        for j in range(CAP):
            row = send[0, j, lists[n]]

            @pl.when(row < NB)
            def _(src=src, j=j, row=row):
                for x in range(8):
                    acc[row * 8 + x] += src[j, x].astype(F32)

    for x in range(8):
        for b in range(NB):
            out[b, x] = (acc[b * 8 + x] * live[b, x].astype(F32)).astype(BF16)


def sum_kernel(parts, *refs, scale):
    out = refs[-1]
    total = parts[0]
    for n in range(1, parts.shape[0]):
        total = total + parts[n]
    total = total * scale
    for n in range(out.shape[0]):
        out[n] = total


def unpack_kernel(packed, out):
    for n in range(14):
        tile = packed[64 * n : 64 * n + 64, :]
        out[2 * n] = tile[:, 0:64]
        if 2 * n + 1 < 27:
            out[2 * n + 1] = pltpu.roll(tile, 64, 1)[:, 0:64]


def in_vmem(x):
    return pltpu.with_memory_space_constraint(x, pltpu.VMEM)


VM = pl.BlockSpec(memory_space=pltpu.VMEM)
SM = pl.BlockSpec(memory_space=pltpu.SMEM)
ANY = pl.BlockSpec(memory_space=pl.ANY)
BLOCK = jax.ShapeDtypeStruct((NB, 8, 8, 512), BF16)
SEND = jax.ShapeDtypeStruct((CAP, 8, 8, 512), BF16)


def call(kernel, name, ins, outs, scratch=(), **params):
    return pl.pallas_call(
        kernel,
        out_shape=outs,
        in_specs=ins,
        out_specs=jax.tree.map(lambda _: VM, outs),
        scratch_shapes=list(scratch),
        name=name,
        **params,
    )


def reduced(parts, copies, scale, name, *before):
    rows = parts.shape[1]
    out = jax.ShapeDtypeStruct((copies, rows, 128), F32)
    kernel = functools.partial(sum_kernel, scale=scale)
    specs = [VM] + [ANY if x.ndim == 4 and x.shape[0] == NB else VM for x in before]
    return call(kernel, name, specs, out)(in_vmem(parts), *before)


def on_device(features, grad_out, occupancy, weight, neighbours, send_rows):
    shape = jax.ShapeDtypeStruct
    column = lax.axis_index("x").reshape(1)
    send_rows = jnp.transpose(send_rows, (0, 2, 1))
    shown, live, *sends = call(
        prep_kernel,
        "prep",
        [VM, VM, SM, SM],
        (BLOCK, BLOCK, SEND, SEND, SEND, SEND),
        [pltpu.VMEM((NB * 64, 512), F32)],
    )(features, occupancy, send_rows, column)

    def swap(n, block):
        return swapped(block, STEPS[n], FIRST[n])

    arrived = [swap(0, sends[0]), swap(1, sends[1])]
    ready = after(grad_out, sends[0])
    g = call(grad_kernel, "grad", [VM, VM], shape((8, 48, 512), BF16))(ready, live)
    w = after(weight, g).reshape(9, 3, 64, 64)
    none = jnp.zeros((9, 1, 64, 64), BF16)
    wp = jnp.concatenate(
        [jnp.concatenate([w, none], axis=1), jnp.concatenate([none, w], axis=1)], axis=3
    ).reshape(36, 64, 128)
    arrived.append(swap(2, after(sends[2], wp)))
    rloc, *backs = call(
        dgrad_kernel,
        "dgrad",
        [VM, VM, SM, SM],
        (shape((NB * 8, 8, 512), F32), SEND, SEND, SEND, SEND),
        [
            pltpu.VMEM((576, 768), BF16),
            pltpu.VMEM((384, 768), BF16),
            pltpu.VMEM((5, 480, 384), F32),
            pltpu.VMEM((NT * 8, 8, 512), F32),
        ],
    )(g, wp, neighbours, column)
    arrived.append(swap(3, after(sends[3], rloc)))
    gext = call(widen_kernel, "widen", [VM], shape((768, 1536), BF16))(after(g, rloc))
    px, dwp = call(
        wgrad_kernel,
        "wgrad",
        [ANY, VM, VM, VM, VM, ANY, VM, SM, SM],
        (shape((640, 1024), BF16), shape((1024, 128), F32)),
        [
            pltpu.VMEM((NT, 8, 8, 512), BF16),
            pltpu.VMEM((256, 1152), F32),
            pltpu.SemaphoreType.DMA((5,)),
        ],
    )(shown, *map(in_vmem, arrived), rloc, gext, neighbours, column)

    count = lax.axis_size(SPACE) * lax.axis_size("dp")
    scale = 1.0 / math.sqrt(count * NB * 512)
    near = lax.axis_size(PLANE)
    far = count // near
    rows = 1024 // near
    with jax.named_scope("scatter"):
        parts = lax.all_to_all(dwp.reshape(near, rows, 128), PLANE, 0, 0, tiled=True)
    backs = [after(back, dwp) for back in backs]
    returned = [swap(0, backs[0]), swap(1, backs[1])]
    output = call(
        conv_kernel,
        "conv",
        [VM] * 3,
        BLOCK,
        [pltpu.VMEM((768, 384), BF16), pltpu.VMEM((4, 512, 384), F32)],
    )(px, wp, live)
    total = reduced(parts, far, 1.0, "near_sum", output, *map(in_vmem, returned))
    with jax.named_scope("swap"):
        parts = lax.all_to_all(total, "z", 0, 0, tiled=True)
    returned.append(swap(2, after(backs[2], total)))
    total = reduced(parts, near, scale, "far_sum", in_vmem(returned[2]))
    with jax.named_scope("gather"):
        packed = lax.all_to_all(total, PLANE, 0, 0, tiled=True).reshape(1024, 128)
    returned.append(swap(3, after(backs[3], total)))
    weight_grad = call(unpack_kernel, "unpack", [VM], shape((27, 64, 64), F32))(in_vmem(packed))
    feature_grad = call(
        final_kernel,
        "final",
        [VM] * 6 + [SM, SM],
        BLOCK,
        [pltpu.VMEM((NB * 8, 8, 512), F32)],
    )(rloc, *map(in_vmem, returned), live, send_rows, column)
    return (output, feature_grad, weight_grad.reshape(3, 3, 3, 64, 64))


def solution(mesh):
    grid = Mesh(mesh.devices.reshape(4, -1, 4, 2), ("y", "z", "x", "dp"))
    every = ("y", "z", "x", "dp")
    return jax.shard_map(
        on_device,
        mesh=grid,
        in_specs=(
            P(every, None, None, None),
            P(every, None, None, None),
            P(every, None),
            P(),
            P(every, None),
            P(every, None, None),
        ),
        out_specs=(P(every, None, None, None), P(every, None, None, None), P()),
        check_vma=False,
    )
```

```python
import functools
import math

import jax
import jax.numpy as jnp
from jax import lax
from jax.experimental import pallas as pl
from jax.experimental.pallas import tpu as pltpu
from jax.sharding import Mesh
from jax.sharding import PartitionSpec as P

STEPS = (1, 1, 2, 2)
FIRST = (0, 1, 0, 1)
OFFSETS = [
    (step_x, step_y, step_z)
    for step_x in (-1, 0, 1)
    for step_y in (-1, 0, 1)
    for step_z in (-1, 0, 1)
    if (step_x, step_y, step_z) != (0, 0, 0)
]
SLOT_OF = {offset: num for num, offset in enumerate(OFFSETS)}
BF16 = jnp.bfloat16
F32 = jnp.float32
NB = 6
CAP = 2
NT = NB + 4 * CAP + 1


SPACE = ("y", "z", "x")
PLANE = ("y", "x", "dp")


def swapped(block, step, first):
    count = lax.axis_size(SPACE)
    route = []
    for i in range(count):
        peer = i + step if (i // step) % 2 == first else i - step
        if 0 <= peer < count:
            route.append((i, peer))
    return lax.ppermute(block, SPACE, route)


def after(value, *others):
    return lax.optimization_barrier((value, *others))[0]


def dot(left, right, left_dim, right_dim):
    dims = (((left_dim,), (right_dim,)), ((), ()))
    return lax.dot_general(left, right, dims, preferred_element_type=F32)


def live_block(occ_row):
    voxel = lax.broadcasted_iota(jnp.int32, (64, 512), 1)
    line = lax.broadcasted_iota(jnp.int32, (64, 512), 0)
    left = jnp.where(voxel // 8 == line, jnp.broadcast_to(occ_row, (64, 512)), 0)
    voxel = lax.broadcasted_iota(jnp.int32, (512, 512), 0)
    lane = lax.broadcasted_iota(jnp.int32, (512, 512), 1)
    spread = jnp.where(voxel % 8 == lane // 64, 1.0, 0.0)
    return dot(left.astype(F32).astype(BF16), spread.astype(BF16), 1, 0)


def lanes(t):
    return slice(128 * t, 128 * t + 128)


def outgoing(column):
    low = column[0] & 1
    high = column[0] >> 1
    return (low, 1 - low, 2 + high, 3 - high)


def incoming(column):
    low, other, high, last = outgoing(column)
    return (1 - low, 1 - other, 5 - high, 5 - last)


def prep_kernel(feat, occ, send, column, shown, live, s0, s1, s2, s3, mask):
    for b in range(NB):
        mask[64 * b : 64 * b + 64, :] = live_block(occ[b : b + 1, :])
    for x in range(8):
        for b in range(NB):
            on = mask[b * 64 + x * 8 : b * 64 + x * 8 + 8, :]
            live[b, x] = on.astype(BF16)
            shown[b, x] = jnp.where(on > 0.5, feat[b, x].astype(F32), 0.0).astype(BF16)
    lists = outgoing(column)
    for n, out in enumerate((s0, s1, s2, s3)):
        for j in range(CAP):
            row = jnp.minimum(send[0, j, lists[n]], NB - 1)
            out[j] = shown[row]


def grad_kernel(grad, live, g):
    for x in range(8):
        for pair in range(NB // 2):
            parts = []
            for b in (2 * pair, 2 * pair + 1):
                on = live[b, x].astype(F32) > 0.5
                parts.append(jnp.where(on, grad[b, x].astype(F32), 0.0))
            g[x, 16 * pair : 16 * pair + 16, :] = jnp.concatenate(parts, axis=0).astype(BF16)


def dgrad_kernel(g, wp, nbr, column, rloc, r0, r1, r2, r3, gext, wbt, dsc, acc):
    gext[0:96, :] = jnp.zeros((96, 768), BF16)
    gext[480:576, :] = jnp.zeros((96, 768), BF16)
    gext[96:480, 0:128] = jnp.zeros((384, 128), BF16)
    gext[96:480, 640:768] = jnp.zeros((384, 128), BF16)
    for x in range(8):
        gext[96 + 48 * x : 144 + 48 * x, 128:640] = g[x]
    for a in range(3):
        for c in range(3):
            for o in range(2):
                for s in range(2):
                    row = c * 128 + (1 - o) * 64
                    wbt[row : row + 64, a * 256 + s * 128 : a * 256 + s * 128 + 128] = wp[
                        (a * 3 + c) * 4 + o + 2 - 2 * s
                    ]
    for q in range(5):
        left = jnp.concatenate(
            [
                gext[(2 - a) * 48 : (2 - a) * 48 + 480, 128 * q : 128 * q + 256]
                for a in range(3)
            ],
            axis=1,
        )
        dsc[q] = dot(left, wbt[...], 1, 1)
    acc[...] = jnp.zeros((NT * 8, 8, 512), F32)
    low = lax.broadcasted_iota(jnp.int32, (8, 128), 1) < 64
    sub = lax.broadcasted_iota(jnp.int32, (8, 128), 0)

    def add_rows(b, offset, xs, tiles):
        def target(oz):
            if (offset[0], offset[1], oz) == (0, 0, 0):
                return b * 8 + xs
            return nbr[b, SLOT_OF[offset[0], offset[1], oz]] * 8 + xs

        row = target(0)
        for t in range(4):
            acc[row, :, lanes(t)] += tiles[t]
        row = target(1)
        acc[row, :, lanes(0)] += jnp.where(low, tiles[4], 0.0)
        row = target(-1)
        acc[row, :, lanes(3)] += jnp.where(low, 0.0, tiles[4])

    def group(xx, ox, xs):
        for b in range(NB):
            base = pl.multiple_of(xx * 48 + b * 8, 8)
            z = []
            for c in range(3):
                d = [dsc[t, pl.ds(base, 8), lanes(c)] for t in range(5)]
                z.append([jnp.where(low, d[t], d[(t + 1) % 5]) for t in range(5)])
            up = [pltpu.roll(v, 7, 0) for v in z[0]]
            down = [pltpu.roll(v, 1, 0) for v in z[2]]
            inner = [
                z[1][t] + jnp.where(sub < 7, up[t], 0.0) + jnp.where(sub > 0, down[t], 0.0)
                for t in range(5)
            ]
            add_rows(b, (ox, 0), xs, inner)
            add_rows(b, (ox, -1), xs, [jnp.where(sub == 7, v, 0.0) for v in up])
            add_rows(b, (ox, 1), xs, [jnp.where(sub == 0, v, 0.0) for v in down])

    group(0, -1, 7)

    def middle(x, carry):
        group(x + 1, 0, x)
        return carry

    lax.fori_loop(0, 8, middle, 0)
    group(9, 1, 0)
    rloc[...] = acc[0 : NB * 8]
    lists = incoming(column)
    for n, out in enumerate((r0, r1, r2, r3)):
        start = NB + CAP * lists[n]
        for j in range(CAP):
            for x in range(8):
                out[j, x] = acc[(start + j) * 8 + x].astype(BF16)


def widen_kernel(g, gext):
    sub = lax.broadcasted_iota(jnp.int32, (8, 128), 0)
    zero = jnp.zeros((8, 128), F32)
    gext[0:128, :] = jnp.zeros((128, 1536), BF16)
    gext[640:768, :] = jnp.zeros((128, 1536), BF16)

    def fill_g(x, carry):
        for p in range(4):
            cols = [p * 384 + c * 128 for c in range(3)]
            h_low, h_high = zero, zero
            base = pl.multiple_of((x + 2) * 64, 64)
            for pair in range(NB // 2):
                both = g[x, 16 * pair : 16 * pair + 16, lanes(p)]
                both32 = both.astype(F32)
                ups, downs = [], []
                for half in range(2):
                    b = 2 * pair + half
                    v = both32[8 * half : 8 * half + 8]
                    ups.append(jnp.where(sub < 7, pltpu.roll(v, 7, 0), 0.0))
                    downs.append(jnp.where(sub > 0, pltpu.roll(v, 1, 0), 0.0))
                    h_low = jnp.where(sub == b, pltpu.roll(v, b, 0) if b else v, h_low)
                    h_high = jnp.where(sub == b, pltpu.roll(v, b + 1, 0), h_high)
                rows = pl.ds(pl.multiple_of(base + 16 * pair, 16), 16)
                gext[rows, cols[0] : cols[0] + 128] = jnp.concatenate(ups, 0).astype(BF16)
                gext[rows, cols[1] : cols[1] + 128] = both
                gext[rows, cols[2] : cols[2] + 128] = jnp.concatenate(downs, 0).astype(BF16)
            rows = pl.ds(pl.multiple_of(base + 48, 16), 16)
            gext[rows, cols[0] : cols[0] + 128] = jnp.concatenate([h_low, zero], 0).astype(BF16)
            gext[rows, cols[1] : cols[1] + 128] = jnp.zeros((16, 128), BF16)
            gext[rows, cols[2] : cols[2] + 128] = jnp.concatenate([zero, h_high], 0).astype(BF16)
        return carry

    lax.fori_loop(0, 8, fill_g, 0)


def wgrad_kernel(shown, a0, a1, a2, a3, before, gext, nbr, column, px, dwp, table, dsc, sems):
    copies = [pltpu.make_async_copy(shown, table.at[0:NB], sems.at[0])]
    lists = incoming(column)
    for n, src in enumerate((a0, a1, a2, a3)):
        start = NB + CAP * lists[n]
        copies.append(pltpu.make_async_copy(src, table.at[pl.ds(start, CAP)], sems.at[n + 1]))
    for copy in copies:
        copy.start()
    low = lax.broadcasted_iota(jnp.int32, (8, 128), 1) < 64
    sub = lax.broadcasted_iota(jnp.int32, (8, 128), 0)
    zero = jnp.zeros((8, 128), F32)
    table[NT - 1] = jnp.zeros((8, 8, 512), BF16)
    for copy in copies:
        copy.wait()

    def windows(tiles):
        merged = [
            jnp.where(low, tiles[p + 1], tiles[(p + 4) % 5]) for p in range(4)
        ]
        return [v for p in range(4) for v in (tiles[p], merged[p])]

    def five(b, ox, oy, xs):
        def source(oz):
            if (ox, oy, oz) == (0, 0, 0):
                return table[b, xs].astype(F32)
            return table[nbr[b, SLOT_OF[ox, oy, oz]], xs].astype(F32)

        centre, after, before = source(0), source(1), source(-1)
        tiles = [centre[:, lanes(t)] for t in range(4)]
        return tiles + [jnp.where(low, after[:, lanes(0)], before[:, lanes(3)])]

    def fill_plane(xx, ox, xs):
        base = pl.multiple_of(xx * 64, 64)
        h_low, h_high = [zero] * 5, [zero] * 5
        for pair in range(NB // 2):
            wins = []
            for b in (2 * pair, 2 * pair + 1):
                wins.append(windows(five(b, ox, 0, xs)))
                v = five(b, ox, -1, xs)
                h_low = [
                    jnp.where(sub == b, pltpu.roll(v[t], b + 1, 0), h_low[t]) for t in range(5)
                ]
                v = five(b, ox, 1, xs)
                h_high = [
                    jnp.where(sub == b, pltpu.roll(v[t], b, 0) if b else v[t], h_high[t])
                    for t in range(5)
                ]
            rows = pl.ds(pl.multiple_of(base + 16 * pair, 16), 16)
            for n in range(8):
                px[rows, lanes(n)] = jnp.concatenate([wins[0][n], wins[1][n]], 0).astype(BF16)
        wins = [windows(h_low), windows(h_high)]
        rows = pl.ds(pl.multiple_of(base + 48, 16), 16)
        for n in range(8):
            px[rows, lanes(n)] = jnp.concatenate([wins[0][n], wins[1][n]], 0).astype(BF16)

    fill_plane(0, -1, 7)

    def middle_fill(x, carry):
        fill_plane(x + 1, 0, x)
        return carry

    lax.fori_loop(0, 8, middle_fill, 0)
    fill_plane(9, 1, 0)

    for p in range(4):
        right = jnp.concatenate(
            [
                gext[(2 - a) * 64 : (2 - a) * 64 + 640, p * 384 : p * 384 + 384]
                for a in range(3)
            ],
            axis=1,
        )
        part = dot(px[:, 256 * p : 256 * p + 256], right, 0, 0)
        if p == 0:
            dsc[...] = part
        else:
            dsc[...] += part
    low64 = lax.broadcasted_iota(jnp.int32, (64, 128), 1) < 64
    row_of = (192, 0, 64, 128)
    taps = [(a, c, e) for a in range(3) for c in range(3) for e in range(3)]

    def tap_parts(tap):
        a, c, e = tap
        col = a * 384 + c * 128
        first = dsc[row_of[e] : row_of[e] + 64, col : col + 128]
        second = dsc[row_of[e + 1] : row_of[e + 1] + 64, col : col + 128]
        return first, second

    for n in range(14):
        first, second = tap_parts(taps[2 * n])
        left = first + pltpu.roll(second, 64, 1)
        if 2 * n + 1 < 27:
            first, second = tap_parts(taps[2 * n + 1])
            right = second + pltpu.roll(first, 64, 1)
        else:
            right = jnp.zeros((64, 128), F32)
        dwp[64 * n : 64 * n + 64, :] = jnp.where(low64, left, right)
    dwp[896:1024, :] = jnp.zeros((128, 128), F32)


def conv_kernel(px, wp, live, out, wf, gsc):
    sub = lax.broadcasted_iota(jnp.int32, (8, 128), 0)
    for a in range(3):
        for c in range(3):
            for n, t in enumerate((1, 2, 3, 0)):
                row = a * 256 + n * 64
                wf[row : row + 64, lanes(c)] = wp[(a * 3 + c) * 4 + t]
    for p in range(4):
        left = jnp.concatenate(
            [px[64 * a : 64 * a + 512, 256 * p : 256 * p + 256] for a in range(3)], axis=1
        )
        gsc[p] = dot(left, wf[...], 1, 0)

    def finish(x, carry):
        base = pl.multiple_of(x * 64, 64)
        for p in range(4):
            lo_rows = gsc[p, pl.ds(pl.multiple_of(base + 48, 8), 8), lanes(0)]
            hi_rows = gsc[p, pl.ds(pl.multiple_of(base + 56, 8), 8), lanes(2)]
            for b in range(NB):
                rows = pl.ds(pl.multiple_of(base + 8 * b, 8), 8)
                v = [gsc[p, rows, lanes(c)] for c in range(3)]
                lo = pltpu.roll(lo_rows, (8 - b) % 8, 0) if b else lo_rows
                hi = pltpu.roll(hi_rows, 7 - b, 0)
                total = (
                    v[1]
                    + jnp.where(sub > 0, pltpu.roll(v[0], 1, 0), lo)
                    + jnp.where(sub < 7, pltpu.roll(v[2], 7, 0), hi)
                )
                on = live[b, x, :, lanes(p)].astype(F32)
                out[b, x, :, lanes(p)] = (total * on).astype(BF16)
        return carry

    lax.fori_loop(0, 8, finish, 0)


def final_kernel(rloc, a0, a1, a2, a3, live, send, column, out, acc):
    acc[...] = rloc[...]
    lists = outgoing(column)
    for n, src in enumerate((a0, a1, a2, a3)):
        for j in range(CAP):
            row = send[0, j, lists[n]]

            @pl.when(row < NB)
            def _(src=src, j=j, row=row):
                for x in range(8):
                    acc[row * 8 + x] += src[j, x].astype(F32)

    for x in range(8):
        for b in range(NB):
            out[b, x] = (acc[b * 8 + x] * live[b, x].astype(F32)).astype(BF16)


def sum_kernel(parts, *refs, scale):
    out = refs[-1]
    total = parts[0]
    for n in range(1, parts.shape[0]):
        total = total + parts[n]
    total = total * scale
    for n in range(out.shape[0]):
        out[n] = total


def unpack_kernel(packed, out):
    for n in range(14):
        tile = packed[64 * n : 64 * n + 64, :]
        out[2 * n] = tile[:, 0:64]
        if 2 * n + 1 < 27:
            out[2 * n + 1] = pltpu.roll(tile, 64, 1)[:, 0:64]


def in_vmem(x):
    return pltpu.with_memory_space_constraint(x, pltpu.VMEM)


VM = pl.BlockSpec(memory_space=pltpu.VMEM)
SM = pl.BlockSpec(memory_space=pltpu.SMEM)
ANY = pl.BlockSpec(memory_space=pl.ANY)
BLOCK = jax.ShapeDtypeStruct((NB, 8, 8, 512), BF16)
HELD = pltpu.VMEM((NB, 8, 8, 512), BF16)
SEND = pltpu.VMEM((CAP, 8, 8, 512), BF16)


def call(kernel, name, ins, outs, scratch=(), **params):
    return pl.pallas_call(
        kernel,
        out_shape=outs,
        in_specs=ins,
        out_specs=[VM] * len(outs) if isinstance(outs, tuple) else VM,
        scratch_shapes=list(scratch),
        compiler_params=pltpu.CompilerParams(vmem_limit_bytes=20 << 20),
        name=name,
        **params,
    )


def reduced(parts, copies, scale, name, *before):
    rows = parts.shape[1]
    out = pltpu.VMEM((copies, rows, 128), F32)
    kernel = functools.partial(sum_kernel, scale=scale)
    specs = [VM] + [ANY if x.ndim == 4 and x.shape[0] == NB else VM for x in before]
    return call(kernel, name, specs, out)(in_vmem(parts), *before)


def on_device(features, grad_out, occupancy, weight, neighbours, send_rows):
    shape = jax.ShapeDtypeStruct
    column = lax.axis_index("x").reshape(1)
    send_rows = jnp.transpose(send_rows, (0, 2, 1))
    shown, live, *sends = call(
        prep_kernel,
        "prep",
        [VM, VM, SM, SM],
        (HELD, HELD, SEND, SEND, SEND, SEND),
        [pltpu.VMEM((NB * 64, 512), F32)],
    )(features, occupancy, send_rows, column)

    def swap(n, block):
        return swapped(block, STEPS[n], FIRST[n])

    arrived = [swap(0, sends[0]), swap(1, sends[1])]
    ready = after(grad_out, sends[0])
    g = call(grad_kernel, "grad", [VM, VM], pltpu.VMEM((8, 48, 512), BF16))(ready, in_vmem(live))
    w = after(weight, g).reshape(9, 3, 64, 64)
    none = jnp.zeros((9, 1, 64, 64), BF16)
    wp = jnp.concatenate(
        [jnp.concatenate([w, none], axis=1), jnp.concatenate([none, w], axis=1)], axis=3
    ).reshape(36, 64, 128)
    arrived.append(swap(2, after(sends[2], wp)))
    rloc, *backs = call(
        dgrad_kernel,
        "dgrad",
        [VM, VM, SM, SM],
        (pltpu.VMEM((NB * 8, 8, 512), F32), SEND, SEND, SEND, SEND),
        [
            pltpu.VMEM((576, 768), BF16),
            pltpu.VMEM((384, 768), BF16),
            pltpu.VMEM((5, 480, 384), F32),
            pltpu.VMEM((NT * 8, 8, 512), F32),
        ],
    )(in_vmem(g), in_vmem(wp), neighbours, column)
    arrived.append(swap(3, after(sends[3], rloc)))
    gext = call(widen_kernel, "widen", [VM], pltpu.VMEM((768, 1536), BF16))(in_vmem(after(g, rloc)))
    px, dwp = call(
        wgrad_kernel,
        "wgrad",
        [VM] * 7 + [SM, SM],
        (pltpu.VMEM((640, 1024), BF16), pltpu.VMEM((1024, 128), F32)),
        [
            pltpu.VMEM((NT, 8, 8, 512), BF16),
            pltpu.VMEM((256, 1152), F32),
            pltpu.SemaphoreType.DMA((5,)),
        ],
    )(in_vmem(shown), *map(in_vmem, arrived), in_vmem(rloc), in_vmem(gext), neighbours, column)

    count = lax.axis_size(SPACE) * lax.axis_size("dp")
    scale = 1.0 / math.sqrt(count * NB * 512)
    near = lax.axis_size(PLANE)
    far = count // near
    rows = 1024 // near
    with jax.named_scope("scatter"):
        parts = lax.all_to_all(dwp.reshape(near, rows, 128), PLANE, 0, 0, tiled=True)
    backs = [after(back, dwp) for back in backs]
    returned = [swap(0, backs[0]), swap(1, backs[1])]
    total = reduced(parts, far, 1.0, "near_sum", *map(in_vmem, returned))
    with jax.named_scope("swap"):
        parts = lax.all_to_all(total, "z", 0, 0, tiled=True)
    returned.append(swap(2, after(backs[2], total)))
    total = reduced(parts, near, scale, "far_sum", in_vmem(returned[2]))
    with jax.named_scope("gather"):
        packed = lax.all_to_all(total, PLANE, 0, 0, tiled=True).reshape(1024, 128)
    returned.append(swap(3, after(backs[3], total)))
    output = call(
        conv_kernel,
        "conv",
        [VM] * 3,
        BLOCK,
        [pltpu.VMEM((768, 384), BF16), pltpu.VMEM((4, 512, 384), F32)],
    )(in_vmem(after(px, total)), in_vmem(wp), in_vmem(live))
    weight_grad = call(unpack_kernel, "unpack", [VM], shape((27, 64, 64), F32))(in_vmem(packed))
    feature_grad = call(
        final_kernel,
        "final",
        [VM] * 6 + [SM, SM],
        BLOCK,
        [pltpu.VMEM((NB * 8, 8, 512), F32)],
    )(in_vmem(rloc), *map(in_vmem, returned), in_vmem(live), send_rows, column)
    return (output, feature_grad, weight_grad.reshape(3, 3, 3, 64, 64))


def solution(mesh):
    grid = Mesh(mesh.devices.reshape(4, -1, 4, 2), ("y", "z", "x", "dp"))
    every = ("y", "z", "x", "dp")
    return jax.shard_map(
        on_device,
        mesh=grid,
        in_specs=(
            P(every, None, None, None),
            P(every, None, None, None),
            P(every, None),
            P(),
            P(every, None),
            P(every, None, None),
        ),
        out_specs=(P(every, None, None, None), P(every, None, None, None), P()),
        check_vma=False,
    )
```

```python
import functools
import math

import jax
import jax.numpy as jnp
from jax import lax
from jax.experimental import pallas as pl
from jax.experimental.pallas import tpu as pltpu
from jax.sharding import Mesh
from jax.sharding import PartitionSpec as P

STEPS = (1, 1, 2, 2)
FIRST = (0, 1, 0, 1)
OFFSETS = [
    (step_x, step_y, step_z)
    for step_x in (-1, 0, 1)
    for step_y in (-1, 0, 1)
    for step_z in (-1, 0, 1)
    if (step_x, step_y, step_z) != (0, 0, 0)
]
SLOT_OF = {offset: num for num, offset in enumerate(OFFSETS)}
BF16 = jnp.bfloat16
F32 = jnp.float32
NB = 6
CAP = 2
NT = NB + 4 * CAP + 1


SPACE = ("y", "z", "x")
PLANE = ("y", "x", "dp")


def swapped(block, step, first):
    count = lax.axis_size(SPACE)
    route = []
    for i in range(count):
        peer = i + step if (i // step) % 2 == first else i - step
        if 0 <= peer < count:
            route.append((i, peer))
    return lax.ppermute(block, SPACE, route)


def after(value, *others):
    return lax.optimization_barrier((value, *others))[0]


def dot(left, right, left_dim, right_dim):
    dims = (((left_dim,), (right_dim,)), ((), ()))
    return lax.dot_general(left, right, dims, preferred_element_type=F32)


def live_block(occ_row):
    voxel = lax.broadcasted_iota(jnp.int32, (64, 512), 1)
    line = lax.broadcasted_iota(jnp.int32, (64, 512), 0)
    left = jnp.where(voxel // 8 == line, jnp.broadcast_to(occ_row, (64, 512)), 0)
    voxel = lax.broadcasted_iota(jnp.int32, (512, 512), 0)
    lane = lax.broadcasted_iota(jnp.int32, (512, 512), 1)
    spread = jnp.where(voxel % 8 == lane // 64, 1.0, 0.0)
    return dot(left.astype(F32).astype(BF16), spread.astype(BF16), 1, 0)


def lanes(t):
    return slice(128 * t, 128 * t + 128)


def outgoing(column):
    low = column[0] & 1
    high = column[0] >> 1
    return (low, 1 - low, 2 + high, 3 - high)


def incoming(column):
    low, other, high, last = outgoing(column)
    return (1 - low, 1 - other, 5 - high, 5 - last)


def prep_kernel(
    feat_far, grad_far, occ_far, send, column, shown, live, g, s0, s1, s2, s3,
    mask, feat, grad, occ, sems,
):
    copies = [pltpu.make_async_copy(occ_far, occ, sems.at[0])]
    for pair in range(NB // 2):
        part = pl.ds(2 * pair, 2)
        copies.append(
            pltpu.make_async_copy(feat_far.at[part], feat.at[part], sems.at[1 + pair])
        )
    copies.append(pltpu.make_async_copy(grad_far, grad, sems.at[1 + NB // 2]))
    for copy in copies:
        copy.start()
    copies[0].wait()
    for b in range(NB):
        mask[64 * b : 64 * b + 64, :] = live_block(occ[b : b + 1, :])
    for b in range(NB):
        if b % 2 == 0:
            copies[1 + b // 2].wait()
        for x in range(8):
            on = mask[b * 64 + x * 8 : b * 64 + x * 8 + 8, :]
            live[b, x] = on.astype(BF16)
            shown[b, x] = jnp.where(on > 0.5, feat[b, x].astype(F32), 0.0).astype(BF16)
    lists = outgoing(column)
    for n, out in enumerate((s0, s1, s2, s3)):
        for j in range(CAP):
            row = jnp.minimum(send[0, j, lists[n]], NB - 1)
            out[j] = shown[row]
    copies[-1].wait()
    for x in range(8):
        for pair in range(NB // 2):
            parts = []
            for b in (2 * pair, 2 * pair + 1):
                on = mask[b * 64 + x * 8 : b * 64 + x * 8 + 8, :] > 0.5
                parts.append(jnp.where(on, grad[b, x].astype(F32), 0.0))
            g[x, 16 * pair : 16 * pair + 16, :] = jnp.concatenate(parts, axis=0).astype(BF16)


def dgrad_kernel(g, wp, nbr, column, rloc, r0, r1, r2, r3, gext, wbt, dsc, acc):
    gext[0:96, :] = jnp.zeros((96, 768), BF16)
    gext[480:576, :] = jnp.zeros((96, 768), BF16)
    gext[96:480, 0:128] = jnp.zeros((384, 128), BF16)
    gext[96:480, 640:768] = jnp.zeros((384, 128), BF16)
    for x in range(8):
        gext[96 + 48 * x : 144 + 48 * x, 128:640] = g[x]
    for a in range(3):
        for c in range(3):
            for o in range(2):
                for s in range(2):
                    row = c * 128 + (1 - o) * 64
                    wbt[row : row + 64, a * 256 + s * 128 : a * 256 + s * 128 + 128] = wp[
                        (a * 3 + c) * 4 + o + 2 - 2 * s
                    ]
    for q in range(5):
        left = jnp.concatenate(
            [
                gext[(2 - a) * 48 : (2 - a) * 48 + 480, 128 * q : 128 * q + 256]
                for a in range(3)
            ],
            axis=1,
        )
        dsc[q] = dot(left, wbt[...], 1, 1)
    acc[...] = jnp.zeros((NT * 8, 8, 512), F32)
    low = lax.broadcasted_iota(jnp.int32, (8, 128), 1) < 64
    sub = lax.broadcasted_iota(jnp.int32, (8, 128), 0)

    def add_rows(b, offset, xs, tiles):
        def target(oz):
            if (offset[0], offset[1], oz) == (0, 0, 0):
                return b * 8 + xs
            return nbr[b, SLOT_OF[offset[0], offset[1], oz]] * 8 + xs

        row = target(0)
        for t in range(4):
            acc[row, :, lanes(t)] += tiles[t]
        row = target(1)
        acc[row, :, lanes(0)] += jnp.where(low, tiles[4], 0.0)
        row = target(-1)
        acc[row, :, lanes(3)] += jnp.where(low, 0.0, tiles[4])

    def group(xx, ox, xs):
        for b in range(NB):
            base = pl.multiple_of(xx * 48 + b * 8, 8)
            z = []
            for c in range(3):
                d = [dsc[t, pl.ds(base, 8), lanes(c)] for t in range(5)]
                z.append([jnp.where(low, d[t], d[(t + 1) % 5]) for t in range(5)])
            up = [pltpu.roll(v, 7, 0) for v in z[0]]
            down = [pltpu.roll(v, 1, 0) for v in z[2]]
            inner = [
                z[1][t] + jnp.where(sub < 7, up[t], 0.0) + jnp.where(sub > 0, down[t], 0.0)
                for t in range(5)
            ]
            add_rows(b, (ox, 0), xs, inner)
            add_rows(b, (ox, -1), xs, [jnp.where(sub == 7, v, 0.0) for v in up])
            add_rows(b, (ox, 1), xs, [jnp.where(sub == 0, v, 0.0) for v in down])

    group(0, -1, 7)

    def middle(x, carry):
        group(x + 1, 0, x)
        return carry

    lax.fori_loop(0, 8, middle, 0)
    group(9, 1, 0)
    rloc[...] = acc[0 : NB * 8]
    lists = incoming(column)
    for n, out in enumerate((r0, r1, r2, r3)):
        start = NB + CAP * lists[n]
        for j in range(CAP):
            for x in range(8):
                out[j, x] = acc[(start + j) * 8 + x].astype(BF16)


def widen_kernel(g, gext):
    sub = lax.broadcasted_iota(jnp.int32, (8, 128), 0)
    zero = jnp.zeros((8, 128), F32)
    gext[0:128, :] = jnp.zeros((128, 1536), BF16)
    gext[640:768, :] = jnp.zeros((128, 1536), BF16)

    def fill_g(x, carry):
        for p in range(4):
            cols = [p * 384 + c * 128 for c in range(3)]
            h_low, h_high = zero, zero
            base = pl.multiple_of((x + 2) * 64, 64)
            for pair in range(NB // 2):
                both = g[x, 16 * pair : 16 * pair + 16, lanes(p)]
                both32 = both.astype(F32)
                ups, downs = [], []
                for half in range(2):
                    b = 2 * pair + half
                    v = both32[8 * half : 8 * half + 8]
                    ups.append(jnp.where(sub < 7, pltpu.roll(v, 7, 0), 0.0))
                    downs.append(jnp.where(sub > 0, pltpu.roll(v, 1, 0), 0.0))
                    h_low = jnp.where(sub == b, pltpu.roll(v, b, 0) if b else v, h_low)
                    h_high = jnp.where(sub == b, pltpu.roll(v, b + 1, 0), h_high)
                rows = pl.ds(pl.multiple_of(base + 16 * pair, 16), 16)
                gext[rows, cols[0] : cols[0] + 128] = jnp.concatenate(ups, 0).astype(BF16)
                gext[rows, cols[1] : cols[1] + 128] = both
                gext[rows, cols[2] : cols[2] + 128] = jnp.concatenate(downs, 0).astype(BF16)
            rows = pl.ds(pl.multiple_of(base + 48, 16), 16)
            gext[rows, cols[0] : cols[0] + 128] = jnp.concatenate([h_low, zero], 0).astype(BF16)
            gext[rows, cols[1] : cols[1] + 128] = jnp.zeros((16, 128), BF16)
            gext[rows, cols[2] : cols[2] + 128] = jnp.concatenate([zero, h_high], 0).astype(BF16)
        return carry

    lax.fori_loop(0, 8, fill_g, 0)


def wgrad_kernel(shown, a0, a1, a2, a3, before, gext, nbr, column, px, dwp, table, dsc, sems):
    copies = [pltpu.make_async_copy(shown, table.at[0:NB], sems.at[0])]
    lists = incoming(column)
    for n, src in enumerate((a0, a1, a2, a3)):
        start = NB + CAP * lists[n]
        copies.append(pltpu.make_async_copy(src, table.at[pl.ds(start, CAP)], sems.at[n + 1]))
    for copy in copies:
        copy.start()
    low = lax.broadcasted_iota(jnp.int32, (8, 128), 1) < 64
    sub = lax.broadcasted_iota(jnp.int32, (8, 128), 0)
    zero = jnp.zeros((8, 128), F32)
    table[NT - 1] = jnp.zeros((8, 8, 512), BF16)
    for copy in copies:
        copy.wait()

    def windows(tiles):
        merged = [
            jnp.where(low, tiles[p + 1], tiles[(p + 4) % 5]) for p in range(4)
        ]
        return [v for p in range(4) for v in (tiles[p], merged[p])]

    def five(b, ox, oy, xs):
        def source(oz):
            if (ox, oy, oz) == (0, 0, 0):
                return table[b, xs].astype(F32)
            return table[nbr[b, SLOT_OF[ox, oy, oz]], xs].astype(F32)

        centre, after, before = source(0), source(1), source(-1)
        tiles = [centre[:, lanes(t)] for t in range(4)]
        return tiles + [jnp.where(low, after[:, lanes(0)], before[:, lanes(3)])]

    def fill_plane(xx, ox, xs):
        base = pl.multiple_of(xx * 64, 64)
        h_low, h_high = [zero] * 5, [zero] * 5
        for pair in range(NB // 2):
            wins = []
            for b in (2 * pair, 2 * pair + 1):
                wins.append(windows(five(b, ox, 0, xs)))
                v = five(b, ox, -1, xs)
                h_low = [
                    jnp.where(sub == b, pltpu.roll(v[t], b + 1, 0), h_low[t]) for t in range(5)
                ]
                v = five(b, ox, 1, xs)
                h_high = [
                    jnp.where(sub == b, pltpu.roll(v[t], b, 0) if b else v[t], h_high[t])
                    for t in range(5)
                ]
            rows = pl.ds(pl.multiple_of(base + 16 * pair, 16), 16)
            for n in range(8):
                px[rows, lanes(n)] = jnp.concatenate([wins[0][n], wins[1][n]], 0).astype(BF16)
        wins = [windows(h_low), windows(h_high)]
        rows = pl.ds(pl.multiple_of(base + 48, 16), 16)
        for n in range(8):
            px[rows, lanes(n)] = jnp.concatenate([wins[0][n], wins[1][n]], 0).astype(BF16)

    fill_plane(0, -1, 7)

    def middle_fill(x, carry):
        fill_plane(x + 1, 0, x)
        return carry

    lax.fori_loop(0, 8, middle_fill, 0)
    fill_plane(9, 1, 0)

    for p in range(4):
        right = jnp.concatenate(
            [
                gext[(2 - a) * 64 : (2 - a) * 64 + 640, p * 384 : p * 384 + 384]
                for a in range(3)
            ],
            axis=1,
        )
        part = dot(px[:, 256 * p : 256 * p + 256], right, 0, 0)
        if p == 0:
            dsc[...] = part
        else:
            dsc[...] += part
    low64 = lax.broadcasted_iota(jnp.int32, (64, 128), 1) < 64
    row_of = (192, 0, 64, 128)
    taps = [(a, c, e) for a in range(3) for c in range(3) for e in range(3)]

    def tap_parts(tap):
        a, c, e = tap
        col = a * 384 + c * 128
        first = dsc[row_of[e] : row_of[e] + 64, col : col + 128]
        second = dsc[row_of[e + 1] : row_of[e + 1] + 64, col : col + 128]
        return first, second

    for n in range(14):
        first, second = tap_parts(taps[2 * n])
        left = first + pltpu.roll(second, 64, 1)
        if 2 * n + 1 < 27:
            first, second = tap_parts(taps[2 * n + 1])
            right = second + pltpu.roll(first, 64, 1)
        else:
            right = jnp.zeros((64, 128), F32)
        dwp[64 * n : 64 * n + 64, :] = jnp.where(low64, left, right)
    dwp[896:1024, :] = jnp.zeros((128, 128), F32)


def conv_kernel(px, wp, live, out, wf, gsc):
    sub = lax.broadcasted_iota(jnp.int32, (8, 128), 0)
    for a in range(3):
        for c in range(3):
            for n, t in enumerate((1, 2, 3, 0)):
                row = a * 256 + n * 64
                wf[row : row + 64, lanes(c)] = wp[(a * 3 + c) * 4 + t]
    for p in range(4):
        left = jnp.concatenate(
            [px[64 * a : 64 * a + 512, 256 * p : 256 * p + 256] for a in range(3)], axis=1
        )
        gsc[p] = dot(left, wf[...], 1, 0)

    def finish(x, carry):
        base = pl.multiple_of(x * 64, 64)
        for p in range(4):
            lo_rows = gsc[p, pl.ds(pl.multiple_of(base + 48, 8), 8), lanes(0)]
            hi_rows = gsc[p, pl.ds(pl.multiple_of(base + 56, 8), 8), lanes(2)]
            for b in range(NB):
                rows = pl.ds(pl.multiple_of(base + 8 * b, 8), 8)
                v = [gsc[p, rows, lanes(c)] for c in range(3)]
                lo = pltpu.roll(lo_rows, (8 - b) % 8, 0) if b else lo_rows
                hi = pltpu.roll(hi_rows, 7 - b, 0)
                total = (
                    v[1]
                    + jnp.where(sub > 0, pltpu.roll(v[0], 1, 0), lo)
                    + jnp.where(sub < 7, pltpu.roll(v[2], 7, 0), hi)
                )
                on = live[b, x, :, lanes(p)].astype(F32)
                out[b, x, :, lanes(p)] = (total * on).astype(BF16)
        return carry

    lax.fori_loop(0, 8, finish, 0)


def final_kernel(rloc, a0, a1, a2, a3, live, send, column, out, acc):
    acc[...] = rloc[...]
    lists = outgoing(column)
    for n, src in enumerate((a0, a1, a2, a3)):
        for j in range(CAP):
            row = send[0, j, lists[n]]

            @pl.when(row < NB)
            def _(src=src, j=j, row=row):
                for x in range(8):
                    acc[row * 8 + x] += src[j, x].astype(F32)

    for x in range(8):
        for b in range(NB):
            out[b, x] = (acc[b * 8 + x] * live[b, x].astype(F32)).astype(BF16)


def sum_kernel(parts, out, *, scale):
    total = parts[0]
    for n in range(1, parts.shape[0]):
        total = total + parts[n]
    total = total * scale
    for n in range(out.shape[0]):
        out[n] = total


def unpack_kernel(packed, out):
    for n in range(14):
        tile = packed[64 * n : 64 * n + 64, :]
        out[2 * n] = tile[:, 0:64]
        if 2 * n + 1 < 27:
            out[2 * n + 1] = pltpu.roll(tile, 64, 1)[:, 0:64]


def in_vmem(x):
    return pltpu.with_memory_space_constraint(x, pltpu.VMEM)


def in_hbm(x):
    return pltpu.with_memory_space_constraint(x, pltpu.HBM)


VM = pl.BlockSpec(memory_space=pltpu.VMEM)
SM = pl.BlockSpec(memory_space=pltpu.SMEM)
HBM = pl.BlockSpec(memory_space=pltpu.HBM)
BLOCK = jax.ShapeDtypeStruct((NB, 8, 8, 512), BF16)
HELD = pltpu.VMEM((NB, 8, 8, 512), BF16)
SEND = pltpu.VMEM((CAP, 8, 8, 512), BF16)


def call(kernel, ins, outs, scratch=(), **params):
    return pl.pallas_call(
        kernel,
        out_shape=outs,
        in_specs=ins,
        out_specs=[VM] * len(outs) if isinstance(outs, tuple) else VM,
        scratch_shapes=list(scratch),
        compiler_params=pltpu.CompilerParams(vmem_limit_bytes=20 << 20),
        **params,
    )


def reduced(parts, copies, scale):
    rows = parts.shape[1]
    out = pltpu.VMEM((copies, rows, 128), F32)
    kernel = functools.partial(sum_kernel, scale=scale)
    return call(kernel, [VM], out)(in_vmem(parts))


def weight_pass(shown, arrived, rloc, gext, neighbours, column):
    shape = jax.ShapeDtypeStruct
    return call(
        wgrad_kernel,
        [VM] * 7 + [SM, SM],
        (shape((640, 1024), BF16), pltpu.VMEM((1024, 128), F32)),
        [
            pltpu.VMEM((NT, 8, 8, 512), BF16),
            pltpu.VMEM((256, 1152), F32),
            pltpu.SemaphoreType.DMA((5,)),
        ],
    )(in_vmem(shown), *map(in_vmem, arrived), in_vmem(rloc), in_vmem(gext), neighbours, column)


def on_device(features, grad_out, occupancy, weight, neighbours, send_rows):
    shape = jax.ShapeDtypeStruct
    column = lax.axis_index("x").reshape(1)
    send_rows = jnp.transpose(send_rows, (0, 2, 1))
    shown, live, g, *sends = call(
        prep_kernel,
        [HBM, HBM, HBM, SM, SM],
        (HELD, HELD, pltpu.VMEM((8, 48, 512), BF16), SEND, SEND, SEND, SEND),
        [
            pltpu.VMEM((NB * 64, 512), F32),
            pltpu.VMEM((NB, 8, 8, 512), BF16),
            pltpu.VMEM((NB, 8, 8, 512), BF16),
            pltpu.VMEM((NB, 512), jnp.int32),
            pltpu.SemaphoreType.DMA((NB // 2 + 2,)),
        ],
    )(in_hbm(features), in_hbm(grad_out), in_hbm(occupancy), send_rows, column)

    def swap(n, block):
        return swapped(block, STEPS[n], FIRST[n])

    arrived = [swap(0, sends[0])]
    arrived.append(swap(1, sends[1]))
    w = weight.reshape(9, 3, 64, 64)
    none = jnp.zeros((9, 1, 64, 64), BF16)
    wp = jnp.concatenate(
        [jnp.concatenate([w, none], axis=1), jnp.concatenate([none, w], axis=1)], axis=3
    ).reshape(36, 64, 128)
    arrived.append(swap(2, after(sends[2], wp)))
    rloc, *backs = call(
        dgrad_kernel,
        [VM, VM, SM, SM],
        (pltpu.VMEM((NB * 8, 8, 512), F32), SEND, SEND, SEND, SEND),
        [
            pltpu.VMEM((576, 768), BF16),
            pltpu.VMEM((384, 768), BF16),
            pltpu.VMEM((5, 480, 384), F32),
            pltpu.VMEM((NT * 8, 8, 512), F32),
        ],
    )(in_vmem(g), in_vmem(wp), neighbours, column)
    arrived.append(swap(3, after(sends[3], rloc)))
    gext = call(widen_kernel, [VM], pltpu.VMEM((768, 1536), BF16))(in_vmem(after(g, rloc)))
    returned = {}
    for n in (0, 2):
        returned[n] = swap(n, after(backs[n], gext))
    px, dwp = weight_pass(shown, arrived, rloc, gext, neighbours, column)

    count = lax.axis_size(SPACE) * lax.axis_size("dp")
    scale = 1.0 / math.sqrt(count * NB * 512)
    near = lax.axis_size(PLANE)
    far = count // near
    rows = 1024 // near
    parts = lax.all_to_all(dwp.reshape(near, rows, 128), PLANE, 0, 0, tiled=True)
    returned[1] = swap(1, after(backs[1], dwp))
    total = reduced(parts, far, 1.0)
    parts = lax.all_to_all(total, "z", 0, 0, tiled=True)
    returned[3] = swap(3, after(backs[3], total))
    total = reduced(parts, near, scale)
    packed = lax.all_to_all(total, PLANE, 0, 0, tiled=True).reshape(1024, 128)
    output = call(
        conv_kernel, [VM] * 3, BLOCK, [pltpu.VMEM((768, 384), BF16), pltpu.VMEM((4, 512, 384), F32)]
    )(in_hbm(px), in_vmem(wp), in_vmem(live))
    weight_grad = call(unpack_kernel, [VM], shape((27, 64, 64), F32))(in_vmem(packed))
    feature_grad = call(
        final_kernel, [VM] * 6 + [SM, SM], BLOCK, [pltpu.VMEM((NB * 8, 8, 512), F32)]
    )(in_vmem(rloc), *(in_vmem(returned[n]) for n in range(4)), in_vmem(live), send_rows, column)
    return (output, feature_grad, weight_grad.reshape(3, 3, 3, 64, 64))


def solution(mesh):
    grid = Mesh(mesh.devices.reshape(4, -1, 4, 2), ("y", "z", "x", "dp"))
    every = ("y", "z", "x", "dp")

    return jax.shard_map(
        on_device,
        mesh=grid,
        in_specs=(
            P(every, None, None, None),
            P(every, None, None, None),
            P(every, None),
            P(),
            P(every, None),
            P(every, None, None),
        ),
        out_specs=(P(every, None, None, None), P(every, None, None, None), P()),
        check_vma=False,
    )
```

```python
import functools
import math

import jax
import jax.numpy as jnp
from jax import lax
from jax.experimental import pallas as pl
from jax.experimental.pallas import tpu as pltpu
from jax.sharding import Mesh
from jax.sharding import PartitionSpec as P

STEPS = (1, 1, 2, 2)
FIRST = (0, 1, 0, 1)
OFFSETS = [
    (step_x, step_y, step_z)
    for step_x in (-1, 0, 1)
    for step_y in (-1, 0, 1)
    for step_z in (-1, 0, 1)
    if (step_x, step_y, step_z) != (0, 0, 0)
]
SLOT_OF = {offset: num for num, offset in enumerate(OFFSETS)}
BF16 = jnp.bfloat16
F32 = jnp.float32
NB = 6
CAP = 2
NT = NB + 4 * CAP + 1


SPACE = ("y", "z", "x")
PLANE = ("y", "x", "dp")


def swapped(block, step, first):
    count = lax.axis_size(SPACE)
    route = []
    for i in range(count):
        peer = i + step if (i // step) % 2 == first else i - step
        if 0 <= peer < count:
            route.append((i, peer))
    return lax.ppermute(block, SPACE, route)


def after(value, *others):
    return lax.optimization_barrier((value, *others))[0]


def dot(left, right, left_dim, right_dim):
    dims = (((left_dim,), (right_dim,)), ((), ()))
    return lax.dot_general(left, right, dims, preferred_element_type=F32)


def live_block(occ_row):
    voxel = lax.broadcasted_iota(jnp.int32, (64, 512), 1)
    line = lax.broadcasted_iota(jnp.int32, (64, 512), 0)
    left = jnp.where(voxel // 8 == line, jnp.broadcast_to(occ_row, (64, 512)), 0)
    voxel = lax.broadcasted_iota(jnp.int32, (512, 512), 0)
    lane = lax.broadcasted_iota(jnp.int32, (512, 512), 1)
    spread = jnp.where(voxel % 8 == lane // 64, 1.0, 0.0)
    return dot(left.astype(F32).astype(BF16), spread.astype(BF16), 1, 0)


def lanes(t):
    return slice(128 * t, 128 * t + 128)


def outgoing(column):
    low = column[0] & 1
    high = column[0] >> 1
    return (low, 1 - low, 2 + high, 3 - high)


def incoming(column):
    low, other, high, last = outgoing(column)
    return (1 - low, 1 - other, 5 - high, 5 - last)


def prep_kernel(
    feat_far, grad_far, occ_far, send, column, shown, live, g, s0, s1, s2, s3,
    mask, feat, grad, occ, sems,
):
    copies = [pltpu.make_async_copy(occ_far, occ, sems.at[0])]
    for pair in range(NB // 2):
        part = pl.ds(2 * pair, 2)
        copies.append(
            pltpu.make_async_copy(feat_far.at[part], feat.at[part], sems.at[1 + pair])
        )
    copies.append(pltpu.make_async_copy(grad_far, grad, sems.at[1 + NB // 2]))
    for copy in copies:
        copy.start()
    copies[0].wait()
    for b in range(NB):
        mask[64 * b : 64 * b + 64, :] = live_block(occ[b : b + 1, :])
    for b in range(NB):
        if b % 2 == 0:
            copies[1 + b // 2].wait()
        for x in range(8):
            on = mask[b * 64 + x * 8 : b * 64 + x * 8 + 8, :]
            live[b, x] = on.astype(BF16)
            shown[b, x] = jnp.where(on > 0.5, feat[b, x].astype(F32), 0.0).astype(BF16)
    lists = outgoing(column)
    for n, out in enumerate((s0, s1, s2, s3)):
        for j in range(CAP):
            row = jnp.minimum(send[0, j, lists[n]], NB - 1)
            out[j] = shown[row]
    copies[-1].wait()
    for x in range(8):
        for pair in range(NB // 2):
            parts = []
            for b in (2 * pair, 2 * pair + 1):
                on = mask[b * 64 + x * 8 : b * 64 + x * 8 + 8, :] > 0.5
                parts.append(jnp.where(on, grad[b, x].astype(F32), 0.0))
            g[x, 16 * pair : 16 * pair + 16, :] = jnp.concatenate(parts, axis=0).astype(BF16)


def dgrad_kernel(g, wp, nbr, column, rloc, r0, r1, r2, r3, gext, wbt, dsc, acc):
    gext[0:96, :] = jnp.zeros((96, 768), BF16)
    gext[480:576, :] = jnp.zeros((96, 768), BF16)
    gext[96:480, 0:128] = jnp.zeros((384, 128), BF16)
    gext[96:480, 640:768] = jnp.zeros((384, 128), BF16)
    for x in range(8):
        gext[96 + 48 * x : 144 + 48 * x, 128:640] = g[x]
    for a in range(3):
        for c in range(3):
            for o in range(2):
                for s in range(2):
                    row = c * 128 + (1 - o) * 64
                    wbt[row : row + 64, a * 256 + s * 128 : a * 256 + s * 128 + 128] = wp[
                        (a * 3 + c) * 4 + o + 2 - 2 * s
                    ]
    for q in range(5):
        left = jnp.concatenate(
            [
                gext[(2 - a) * 48 : (2 - a) * 48 + 480, 128 * q : 128 * q + 256]
                for a in range(3)
            ],
            axis=1,
        )
        dsc[q] = dot(left, wbt[...], 1, 1)
    acc[...] = jnp.zeros((NT * 8, 8, 512), F32)
    low = lax.broadcasted_iota(jnp.int32, (8, 128), 1) < 64
    sub = lax.broadcasted_iota(jnp.int32, (8, 128), 0)

    def add_rows(b, offset, xs, tiles):
        def target(oz):
            if (offset[0], offset[1], oz) == (0, 0, 0):
                return b * 8 + xs
            return nbr[b, SLOT_OF[offset[0], offset[1], oz]] * 8 + xs

        row = target(0)
        for t in range(4):
            acc[row, :, lanes(t)] += tiles[t]
        row = target(1)
        acc[row, :, lanes(0)] += jnp.where(low, tiles[4], 0.0)
        row = target(-1)
        acc[row, :, lanes(3)] += jnp.where(low, 0.0, tiles[4])

    def group(xx, ox, xs):
        for b in range(NB):
            base = pl.multiple_of(xx * 48 + b * 8, 8)
            z = []
            for c in range(3):
                d = [dsc[t, pl.ds(base, 8), lanes(c)] for t in range(5)]
                z.append([jnp.where(low, d[t], d[(t + 1) % 5]) for t in range(5)])
            up = [pltpu.roll(v, 7, 0) for v in z[0]]
            down = [pltpu.roll(v, 1, 0) for v in z[2]]
            inner = [
                z[1][t] + jnp.where(sub < 7, up[t], 0.0) + jnp.where(sub > 0, down[t], 0.0)
                for t in range(5)
            ]
            add_rows(b, (ox, 0), xs, inner)
            add_rows(b, (ox, -1), xs, [jnp.where(sub == 7, v, 0.0) for v in up])
            add_rows(b, (ox, 1), xs, [jnp.where(sub == 0, v, 0.0) for v in down])

    group(0, -1, 7)

    def middle(x, carry):
        group(x + 1, 0, x)
        return carry

    lax.fori_loop(0, 8, middle, 0)
    group(9, 1, 0)
    rloc[...] = acc[0 : NB * 8]
    lists = incoming(column)
    for n, out in enumerate((r0, r1, r2, r3)):
        start = NB + CAP * lists[n]
        for j in range(CAP):
            for x in range(8):
                out[j, x] = acc[(start + j) * 8 + x].astype(BF16)


def widen_kernel(g, gext):
    sub = lax.broadcasted_iota(jnp.int32, (8, 128), 0)
    zero = jnp.zeros((8, 128), F32)
    gext[0:128, :] = jnp.zeros((128, 1536), BF16)
    gext[640:768, :] = jnp.zeros((128, 1536), BF16)

    def fill_g(x, carry):
        for p in range(4):
            cols = [p * 384 + c * 128 for c in range(3)]
            h_low, h_high = zero, zero
            base = pl.multiple_of((x + 2) * 64, 64)
            for pair in range(NB // 2):
                both = g[x, 16 * pair : 16 * pair + 16, lanes(p)]
                both32 = both.astype(F32)
                ups, downs = [], []
                for half in range(2):
                    b = 2 * pair + half
                    v = both32[8 * half : 8 * half + 8]
                    ups.append(jnp.where(sub < 7, pltpu.roll(v, 7, 0), 0.0))
                    downs.append(jnp.where(sub > 0, pltpu.roll(v, 1, 0), 0.0))
                    h_low = jnp.where(sub == b, pltpu.roll(v, b, 0) if b else v, h_low)
                    h_high = jnp.where(sub == b, pltpu.roll(v, b + 1, 0), h_high)
                rows = pl.ds(pl.multiple_of(base + 16 * pair, 16), 16)
                gext[rows, cols[0] : cols[0] + 128] = jnp.concatenate(ups, 0).astype(BF16)
                gext[rows, cols[1] : cols[1] + 128] = both
                gext[rows, cols[2] : cols[2] + 128] = jnp.concatenate(downs, 0).astype(BF16)
            rows = pl.ds(pl.multiple_of(base + 48, 16), 16)
            gext[rows, cols[0] : cols[0] + 128] = jnp.concatenate([h_low, zero], 0).astype(BF16)
            gext[rows, cols[1] : cols[1] + 128] = jnp.zeros((16, 128), BF16)
            gext[rows, cols[2] : cols[2] + 128] = jnp.concatenate([zero, h_high], 0).astype(BF16)
        return carry

    lax.fori_loop(0, 8, fill_g, 0)


def wgrad_kernel(shown, a0, a1, a2, a3, before, gext, nbr, column, px, dwp, table, dsc, sems):
    copies = [pltpu.make_async_copy(shown, table.at[0:NB], sems.at[0])]
    lists = incoming(column)
    for n, src in enumerate((a0, a1, a2, a3)):
        start = NB + CAP * lists[n]
        copies.append(pltpu.make_async_copy(src, table.at[pl.ds(start, CAP)], sems.at[n + 1]))
    for copy in copies:
        copy.start()
    low = lax.broadcasted_iota(jnp.int32, (8, 128), 1) < 64
    sub = lax.broadcasted_iota(jnp.int32, (8, 128), 0)
    zero = jnp.zeros((8, 128), F32)
    table[NT - 1] = jnp.zeros((8, 8, 512), BF16)
    for copy in copies:
        copy.wait()

    def windows(tiles):
        merged = [
            jnp.where(low, tiles[p + 1], tiles[(p + 4) % 5]) for p in range(4)
        ]
        return [v for p in range(4) for v in (tiles[p], merged[p])]

    def five(b, ox, oy, xs):
        def source(oz):
            if (ox, oy, oz) == (0, 0, 0):
                return table[b, xs].astype(F32)
            return table[nbr[b, SLOT_OF[ox, oy, oz]], xs].astype(F32)

        centre, after, before = source(0), source(1), source(-1)
        tiles = [centre[:, lanes(t)] for t in range(4)]
        return tiles + [jnp.where(low, after[:, lanes(0)], before[:, lanes(3)])]

    def fill_plane(xx, ox, xs):
        base = pl.multiple_of(xx * 64, 64)
        h_low, h_high = [zero] * 5, [zero] * 5
        for pair in range(NB // 2):
            wins = []
            for b in (2 * pair, 2 * pair + 1):
                wins.append(windows(five(b, ox, 0, xs)))
                v = five(b, ox, -1, xs)
                h_low = [
                    jnp.where(sub == b, pltpu.roll(v[t], b + 1, 0), h_low[t]) for t in range(5)
                ]
                v = five(b, ox, 1, xs)
                h_high = [
                    jnp.where(sub == b, pltpu.roll(v[t], b, 0) if b else v[t], h_high[t])
                    for t in range(5)
                ]
            rows = pl.ds(pl.multiple_of(base + 16 * pair, 16), 16)
            for n in range(8):
                px[rows, lanes(n)] = jnp.concatenate([wins[0][n], wins[1][n]], 0).astype(BF16)
        wins = [windows(h_low), windows(h_high)]
        rows = pl.ds(pl.multiple_of(base + 48, 16), 16)
        for n in range(8):
            px[rows, lanes(n)] = jnp.concatenate([wins[0][n], wins[1][n]], 0).astype(BF16)

    fill_plane(0, -1, 7)

    def middle_fill(x, carry):
        fill_plane(x + 1, 0, x)
        return carry

    lax.fori_loop(0, 8, middle_fill, 0)
    fill_plane(9, 1, 0)

    for p in range(4):
        right = jnp.concatenate(
            [
                gext[(2 - a) * 64 : (2 - a) * 64 + 640, p * 384 : p * 384 + 384]
                for a in range(3)
            ],
            axis=1,
        )
        part = dot(px[:, 256 * p : 256 * p + 256], right, 0, 0)
        if p == 0:
            dsc[...] = part
        else:
            dsc[...] += part
    low64 = lax.broadcasted_iota(jnp.int32, (64, 128), 1) < 64
    row_of = (192, 0, 64, 128)
    taps = [(a, c, e) for a in range(3) for c in range(3) for e in range(3)]

    def tap_parts(tap):
        a, c, e = tap
        col = a * 384 + c * 128
        first = dsc[row_of[e] : row_of[e] + 64, col : col + 128]
        second = dsc[row_of[e + 1] : row_of[e + 1] + 64, col : col + 128]
        return first, second

    for n in range(14):
        first, second = tap_parts(taps[2 * n])
        left = first + pltpu.roll(second, 64, 1)
        if 2 * n + 1 < 27:
            first, second = tap_parts(taps[2 * n + 1])
            right = second + pltpu.roll(first, 64, 1)
        else:
            right = jnp.zeros((64, 128), F32)
        dwp[64 * n : 64 * n + 64, :] = jnp.where(low64, left, right)
    dwp[896:1024, :] = jnp.zeros((128, 128), F32)


def conv_kernel(px, wp, live, out, wf, gsc):
    sub = lax.broadcasted_iota(jnp.int32, (8, 128), 0)
    for a in range(3):
        for c in range(3):
            for n, t in enumerate((1, 2, 3, 0)):
                row = a * 256 + n * 64
                wf[row : row + 64, lanes(c)] = wp[(a * 3 + c) * 4 + t]
    for p in range(4):
        left = jnp.concatenate(
            [px[64 * a : 64 * a + 512, 256 * p : 256 * p + 256] for a in range(3)], axis=1
        )
        gsc[p] = dot(left, wf[...], 1, 0)

    def finish(x, carry):
        base = pl.multiple_of(x * 64, 64)
        for p in range(4):
            lo_rows = gsc[p, pl.ds(pl.multiple_of(base + 48, 8), 8), lanes(0)]
            hi_rows = gsc[p, pl.ds(pl.multiple_of(base + 56, 8), 8), lanes(2)]
            for b in range(NB):
                rows = pl.ds(pl.multiple_of(base + 8 * b, 8), 8)
                v = [gsc[p, rows, lanes(c)] for c in range(3)]
                lo = pltpu.roll(lo_rows, (8 - b) % 8, 0) if b else lo_rows
                hi = pltpu.roll(hi_rows, 7 - b, 0)
                total = (
                    v[1]
                    + jnp.where(sub > 0, pltpu.roll(v[0], 1, 0), lo)
                    + jnp.where(sub < 7, pltpu.roll(v[2], 7, 0), hi)
                )
                on = live[b, x, :, lanes(p)].astype(F32)
                out[b, x, :, lanes(p)] = (total * on).astype(BF16)
        return carry

    lax.fori_loop(0, 8, finish, 0)


def final_kernel(rloc, a0, a1, a2, a3, live, send, column, out, acc):
    acc[...] = rloc[...]
    lists = outgoing(column)
    for n, src in enumerate((a0, a1, a2, a3)):
        for j in range(CAP):
            row = send[0, j, lists[n]]

            @pl.when(row < NB)
            def _(src=src, j=j, row=row):
                for x in range(8):
                    acc[row * 8 + x] += src[j, x].astype(F32)

    for x in range(8):
        for b in range(NB):
            out[b, x] = (acc[b * 8 + x] * live[b, x].astype(F32)).astype(BF16)


def sum_kernel(parts, out, *, scale):
    total = parts[0]
    for n in range(1, parts.shape[0]):
        total = total + parts[n]
    total = (total * scale).astype(out.dtype)
    for n in range(out.shape[0]):
        out[n] = total


def unpack_kernel(packed, out):
    for n in range(14):
        tile = packed[64 * n : 64 * n + 64, :].astype(F32)
        out[2 * n] = tile[:, 0:64]
        if 2 * n + 1 < 27:
            out[2 * n + 1] = pltpu.roll(tile, 64, 1)[:, 0:64]


def in_vmem(x):
    return pltpu.with_memory_space_constraint(x, pltpu.VMEM)


def in_hbm(x):
    return pltpu.with_memory_space_constraint(x, pltpu.HBM)


VM = pl.BlockSpec(memory_space=pltpu.VMEM)
SM = pl.BlockSpec(memory_space=pltpu.SMEM)
HBM = pl.BlockSpec(memory_space=pltpu.HBM)
BLOCK = jax.ShapeDtypeStruct((NB, 8, 8, 512), BF16)
HELD = pltpu.VMEM((NB, 8, 8, 512), BF16)
SEND = pltpu.VMEM((CAP, 8, 8, 512), BF16)


def call(kernel, ins, outs, scratch=(), **params):
    return pl.pallas_call(
        kernel,
        out_shape=outs,
        in_specs=ins,
        out_specs=[VM] * len(outs) if isinstance(outs, tuple) else VM,
        scratch_shapes=list(scratch),
        compiler_params=pltpu.CompilerParams(vmem_limit_bytes=20 << 20),
        **params,
    )


def reduced(parts, copies, scale, dtype):
    rows = parts.shape[1]
    out = pltpu.VMEM((copies, rows, 128), dtype)
    kernel = functools.partial(sum_kernel, scale=scale)
    return call(kernel, [VM], out)(in_vmem(parts))


def weight_pass(shown, arrived, rloc, gext, neighbours, column):
    shape = jax.ShapeDtypeStruct
    return call(
        wgrad_kernel,
        [VM] * 7 + [SM, SM],
        (shape((640, 1024), BF16), pltpu.VMEM((1024, 128), F32)),
        [
            pltpu.VMEM((NT, 8, 8, 512), BF16),
            pltpu.VMEM((256, 1152), F32),
            pltpu.SemaphoreType.DMA((5,)),
        ],
    )(in_vmem(shown), *map(in_vmem, arrived), in_vmem(rloc), in_vmem(gext), neighbours, column)


def on_device(features, grad_out, occupancy, weight, neighbours, send_rows):
    shape = jax.ShapeDtypeStruct
    column = lax.axis_index("x").reshape(1)
    send_rows = jnp.transpose(send_rows, (0, 2, 1))
    shown, live, g, *sends = call(
        prep_kernel,
        [HBM, HBM, HBM, SM, SM],
        (HELD, HELD, pltpu.VMEM((8, 48, 512), BF16), SEND, SEND, SEND, SEND),
        [
            pltpu.VMEM((NB * 64, 512), F32),
            pltpu.VMEM((NB, 8, 8, 512), BF16),
            pltpu.VMEM((NB, 8, 8, 512), BF16),
            pltpu.VMEM((NB, 512), jnp.int32),
            pltpu.SemaphoreType.DMA((NB // 2 + 2,)),
        ],
    )(in_hbm(features), in_hbm(grad_out), in_hbm(occupancy), send_rows, column)

    def swap(n, block):
        return swapped(block, STEPS[n], FIRST[n])

    arrived = [swap(0, sends[0])]
    arrived.append(swap(1, sends[1]))
    w = weight.reshape(9, 3, 64, 64)
    none = jnp.zeros((9, 1, 64, 64), BF16)
    wp = jnp.concatenate(
        [jnp.concatenate([w, none], axis=1), jnp.concatenate([none, w], axis=1)], axis=3
    ).reshape(36, 64, 128)
    arrived.append(swap(2, after(sends[2], wp)))
    rloc, *backs = call(
        dgrad_kernel,
        [VM, VM, SM, SM],
        (pltpu.VMEM((NB * 8, 8, 512), F32), SEND, SEND, SEND, SEND),
        [
            pltpu.VMEM((576, 768), BF16),
            pltpu.VMEM((384, 768), BF16),
            pltpu.VMEM((5, 480, 384), F32),
            pltpu.VMEM((NT * 8, 8, 512), F32),
        ],
    )(in_vmem(g), in_vmem(wp), neighbours, column)
    arrived.append(swap(3, after(sends[3], rloc)))
    gext = call(widen_kernel, [VM], pltpu.VMEM((768, 1536), BF16))(in_vmem(after(g, rloc)))
    returned = {}
    for n in (0, 2):
        returned[n] = swap(n, after(backs[n], gext))
    px, dwp = weight_pass(shown, arrived, rloc, gext, neighbours, column)

    count = lax.axis_size(SPACE) * lax.axis_size("dp")
    scale = 1.0 / math.sqrt(count * NB * 512)
    near = lax.axis_size(PLANE)
    far = count // near
    rows = 1024 // near
    parts = lax.all_to_all(dwp.reshape(near, rows, 128), PLANE, 0, 0, tiled=True)
    returned[1] = swap(1, after(backs[1], dwp))
    total = reduced(parts, far, 1.0, F32)
    parts = lax.all_to_all(total, "z", 0, 0, tiled=True)
    returned[3] = swap(3, after(backs[3], total))
    total = reduced(parts, near, scale, BF16)
    packed = lax.all_to_all(total, PLANE, 0, 0, tiled=True).reshape(1024, 128)
    output = call(
        conv_kernel, [VM] * 3, BLOCK, [pltpu.VMEM((768, 384), BF16), pltpu.VMEM((4, 512, 384), F32)]
    )(in_hbm(px), in_vmem(wp), in_vmem(live))
    weight_grad = call(unpack_kernel, [VM], shape((27, 64, 64), F32))(in_vmem(packed))
    feature_grad = call(
        final_kernel, [VM] * 6 + [SM, SM], BLOCK, [pltpu.VMEM((NB * 8, 8, 512), F32)]
    )(in_vmem(rloc), *(in_vmem(returned[n]) for n in range(4)), in_vmem(live), send_rows, column)
    return (output, feature_grad, weight_grad.reshape(3, 3, 3, 64, 64))


def solution(mesh):
    grid = Mesh(mesh.devices.reshape(4, -1, 4, 2), ("y", "z", "x", "dp"))
    every = ("y", "z", "x", "dp")

    return jax.shard_map(
        on_device,
        mesh=grid,
        in_specs=(
            P(every, None, None, None),
            P(every, None, None, None),
            P(every, None),
            P(),
            P(every, None),
            P(every, None, None),
        ),
        out_specs=(P(every, None, None, None), P(every, None, None, None), P()),
        check_vma=False,
    )
```
